128 devices in a mesh: tm: 2 (over core), cell: 64 (over z, y, x).
Axes of the slice: x: 4, y: 4, z: 4, core: 2. Of those that a mesh axis runs over, the one named last changes fastest.
Arguments:
- block_rows: int32 [2, 4096], P('tm', 'cell'), may hold values from 0 to 255, as said below
- block_cols: int32 [2, 4096], P('tm', 'cell'), may hold values from 0 to 255, as said below
- block_values: bfloat16 [2, 4096, 128, 128], P('tm', 'cell'), as said below
- growth: float32 [2, 32768], P('tm', 'cell'), may hold values from 0.5 to 4
- first_labels: int32 [8, 32768], P(None, 'cell'), may hold values from 0 to 15, as said below
- last_labels: int32 [8, 32768], P(None, 'cell'), may hold values from 0 to 15
Outputs:
- forward_mass: bfloat16 [2, 128, 32768], P('tm', None, 'cell')
- fate: bfloat16 [2, 128, 32768], P('tm', None, 'cell')
The draws below stay inside these ranges and needn't reach their ends.
Inputs may be any that keep to these rules, and one draw needn't show every extreme that they name: `block_rows`: the slots n of a coupling with n // 64 = c name row blocks c * 4 to (c + 1) * 4 - 1 only, and each row block is named by exactly 16 slots of each coupling. `block_cols`: A slot's column block differs from its row block by at most 4; a pair of row and column block may stand in several slots, whose blocks then add. `block_values`: every entry is positive. `first_labels`: in every panel each of the 16 types labels exactly 2048 cells.
All inputs are finite; a program needn't handle non-finite values.
Results may differ from the reference program's by a relative error of at most 0.006.
Values may be sent and summed in bfloat16 or wider, within the bound.
A program may use at most 64 MiB of HBM per device.

```python
import math
import jax
import jax.numpy as jnp
from jax import lax

CELL_TYPES = 16
BLOCK_SIDE = 128
PER_ROW = 16
BAND_REACH = 4
DEV_BLOCKS = 4
PANELS = 8
ALL_CELLS = 32768
TIME_BLOCKS = 256
DEV_SLOTS = 64
ALL_SLOTS = 4096
COUPLINGS = 2
COLUMNS = 128
N_CELL = 64


def band_pairs(key):
    rows_key = jax.random.fold_in(key, 11)
    offset_key = jax.random.fold_in(key, 12)
    keys = jax.random.split(rows_key, COUPLINGS * N_CELL)

    def one_order(one_key):
        return jax.random.permutation(one_key, DEV_SLOTS)
    orders = jax.vmap(one_order)(keys).reshape(COUPLINGS, N_CELL, DEV_SLOTS)
    owner = jnp.arange(N_CELL, dtype=jnp.int32)[None, :, None]
    row_ids = (owner * DEV_BLOCKS + orders // PER_ROW).reshape(COUPLINGS, ALL_SLOTS).astype(jnp.int32)
    offsets = jax.random.randint(offset_key, (COUPLINGS, ALL_SLOTS), -BAND_REACH, BAND_REACH + 1)
    col_ids = row_ids + offsets
    col_ids = jnp.where(col_ids < 0, -col_ids, col_ids)
    col_ids = jnp.where(col_ids > TIME_BLOCKS - 1, 2 * (TIME_BLOCKS - 1) - col_ids, col_ids)
    return (row_ids, col_ids.astype(jnp.int32))


def draw_block_rows(key, part):
    row_ids, col_ids = band_pairs(key)
    return row_ids


def draw_block_cols(key, part):
    row_ids, col_ids = band_pairs(key)
    return col_ids


def draw_block_values(key, part):
    row_ids, col_ids = band_pairs(key)
    value_key = jax.random.fold_in(key, 21)
    col_key = jax.random.fold_in(key, 23)
    full_shape = (COUPLINGS, ALL_SLOTS, BLOCK_SIDE, BLOCK_SIDE)
    rise = 1.0 + 2.0 * col_ids.astype(jnp.float32) / (TIME_BLOCKS - 1)
    col_scale = jnp.exp(jax.random.uniform(col_key, (COUPLINGS, ALL_SLOTS, 1, BLOCK_SIDE), jnp.float32, 0.0, math.log(10.0)))
    entries = jnp.exp(jax.random.uniform(value_key, full_shape, jnp.float32, math.log(0.05), 0.0))
    scaled = entries * col_scale * rise[:, :, None, None] / (PER_ROW * BLOCK_SIDE)
    return scaled.astype(jnp.bfloat16)


def draw_first_labels(key, part):
    keys = jax.random.split(jax.random.fold_in(key, 31), PANELS)

    def one_panel(one_key):
        return jax.random.permutation(one_key, ALL_CELLS) % CELL_TYPES
    return jax.vmap(one_panel)(keys).astype(jnp.int32)


def place_ends(array, stream_key, smallest, high):
    spot = [jax.random.randint(jax.random.fold_in(stream_key, axis), (), 0, length) for axis, length in enumerate(array.shape)]
    longest = array.shape.index(max(array.shape))
    next_to = spot[:longest] + [(spot[longest] + 1) % array.shape[longest]] + spot[longest + 1:]
    return array.at[tuple(spot)].set(smallest).at[tuple(next_to)].set(high)


def steps_of(key, extent, shards, low, high):
    loudness, own = 1.0, jax.random.fold_in(key, 6)
    for position, parts in shards:
        draws = jnp.exp(jax.random.uniform(jax.random.fold_in(own, position), (parts,), jnp.float32, low / len(shards), high / len(shards)))
        loudness = loudness * jnp.repeat(draws, extent[position] // parts).reshape([-1 if axis == position else 1 for axis in range(len(extent))])
    return loudness


def setup_inputs(seed: int = 0) -> dict:
    key_list = jax.random.split(jax.random.key(seed), 7)
    return {
        "block_rows": draw_block_rows(jax.random.fold_in(key_list[6], 71), 0),
        "block_cols": draw_block_cols(jax.random.fold_in(key_list[6], 71), 0),
        "block_values": draw_block_values(jax.random.fold_in(key_list[6], 71), 0),
        "growth": jnp.clip(jnp.exp(math.log(4.0) - 2.0794415 * jax.random.uniform(key_list[3], (COUPLINGS, ALL_CELLS), jnp.float32) ** steps_of(key_list[3], (COUPLINGS, ALL_CELLS), ((0, 2), (1, 64)), -0.2, 0.2)), 0.5, 4.0),
        "first_labels": draw_first_labels(jax.random.fold_in(key_list[6], 71), 0),
        "last_labels": place_ends(jax.random.randint(key_list[5], (PANELS, ALL_CELLS), 0, CELL_TYPES), jax.random.fold_in(key_list[5], 1), 0, CELL_TYPES - 1).astype(jnp.int32),
    }


def seed_stack(labels):
    marks = labels[:, None, :] == jnp.arange(CELL_TYPES, dtype=jnp.int32)[None, :, None]
    return marks.astype(jnp.bfloat16).reshape(COLUMNS, ALL_CELLS)


def forward_step(stack_in, row_ids, col_ids, blocks, growth_row):
    scaled = (stack_in.astype(jnp.float32) / growth_row[None, :]).astype(jnp.bfloat16)
    picked = scaled.reshape(COLUMNS, TIME_BLOCKS, BLOCK_SIDE)[:, row_ids, :]
    carried = jnp.einsum("qsk,skl->qsl", picked.astype(jnp.float32), blocks.astype(jnp.float32))
    summed = jnp.zeros((COLUMNS, TIME_BLOCKS, BLOCK_SIDE), jnp.float32).at[:, col_ids, :].add(carried)
    totals = jnp.sum(summed, axis=(1, 2))
    return (summed * (ALL_CELLS / totals)[:, None, None]).astype(jnp.bfloat16).reshape(COLUMNS, ALL_CELLS)


def backward_step(stack_in, row_ids, col_ids, blocks):
    picked = stack_in.reshape(COLUMNS, TIME_BLOCKS, BLOCK_SIDE)[:, col_ids, :]
    pulled = jnp.einsum("skl,qsl->qsk", blocks.astype(jnp.float32), picked.astype(jnp.float32))
    summed = jnp.zeros((COLUMNS, TIME_BLOCKS, BLOCK_SIDE), jnp.float32).at[:, row_ids, :].add(pulled)
    grouped = summed.reshape(PANELS, CELL_TYPES, TIME_BLOCKS, BLOCK_SIDE)
    fates = grouped * (CELL_TYPES / jnp.sum(grouped, axis=1, keepdims=True))
    return fates.astype(jnp.bfloat16).reshape(COLUMNS, ALL_CELLS)


def reference(block_rows, block_cols, block_values, growth, first_labels, last_labels):
    def forward_turn(stack_in, inputs):
        result = forward_step(stack_in, inputs[0], inputs[1], inputs[2], inputs[3])
        return result, result

    final_mass, forward_mass = lax.scan(forward_turn, seed_stack(first_labels), (block_rows, block_cols, block_values, growth))

    def backward_turn(stack_in, inputs):
        result = backward_step(stack_in, inputs[0], inputs[1], inputs[2])
        return result, result

    first_fate, fate = lax.scan(backward_turn, seed_stack(last_labels), (block_rows, block_cols, block_values), reverse=True)
    return forward_mass, fate
```

```python
import functools

import jax
import jax.numpy as jnp
from jax import lax
from jax.experimental import pallas as pl
from jax.experimental.pallas import tpu as pltpu
from jax.sharding import PartitionSpec as P

CELL_TYPES = 16
BAND_REACH = 4
GROUP = 4
MESH = pl.DeviceIdType.MESH
F32 = jnp.float32
BF16 = jnp.bfloat16


def make_tables(rows, cols, first_block, dev_blocks, per_row, steps, table):
    slots = rows.shape[1]
    lanes = table.shape[1]
    local_row = rows - first_block
    window_col = cols - first_block + BAND_REACH
    down = lax.broadcasted_iota(jnp.int32, (slots, slots), 0)
    across = lax.broadcasted_iota(jnp.int32, (slots, slots), 1)

    def upright(line):
        return jnp.sum(jnp.where(down == across, line, 0), axis=1, keepdims=True)

    row_of, col_of = upright(local_row), upright(window_col)
    earlier = across < down
    in_col = jnp.sum(jnp.where(earlier & (window_col == col_of), 1, 0), axis=1, keepdims=True)
    in_row = jnp.sum(jnp.where(earlier & (local_row == row_of), 1, 0), axis=1, keepdims=True)
    lane = lax.broadcasted_iota(jnp.int32, (slots, lanes), 1)
    slot = lax.broadcasted_iota(jnp.int32, (slots, lanes), 0)
    named = col_of == lane
    count = jnp.sum(jnp.where(named, 1, 0), axis=0, keepdims=True)
    groups = (count + (GROUP - 1)) // GROUP
    base = jnp.sum(jnp.where(lane < col_of, groups, 0), axis=1, keepdims=True)
    place = GROUP * base + in_col
    group_of = base + in_col // GROUP
    hit = place == lane
    group_hit = group_of == lane
    before_hit = group_of == lane - 1
    here = jnp.max(jnp.where(group_hit, col_of, -1), axis=0, keepdims=True)
    before = jnp.max(jnp.where(before_hit, col_of, -2), axis=0, keepdims=True)
    row_place = per_row * row_of + in_row
    row_hit = row_place == lane
    lines = (
        jnp.sum(jnp.where(hit, slot, 0), axis=0, keepdims=True),
        jnp.sum(jnp.where(hit, row_of - dev_blocks, 0), axis=0, keepdims=True) + dev_blocks,
        jnp.where(here == before, 1, 0),
        jnp.max(jnp.where(named, group_of, 0), axis=0, keepdims=True),
        jnp.where(count > 0, 1, 0),
        jnp.sum(jnp.where(row_hit, slot, 0), axis=0, keepdims=True),
        jnp.sum(jnp.where(row_hit, col_of, 0), axis=0, keepdims=True),
        jnp.zeros_like(count),
    )
    bounds = (slots - 1, dev_blocks, 1, steps - 1, 1, slots - 1, dev_blocks + 2 * BAND_REACH - 1, 0)
    lines = [jnp.clip(line, 0, bound) for line, bound in zip(lines, bounds)]
    table[...] = jnp.concatenate(lines, axis=0)


def one_hot(labels):
    panels, side = labels.shape
    kind = lax.broadcasted_iota(jnp.int32, (panels, CELL_TYPES, side), 1)
    marks = jnp.where(labels[:, None, :] == kind, 1.0, 0.0)
    return marks.reshape(panels * CELL_TYPES, side)


def kernel(
    rows_hbm, cols_hbm, blocks_hbm, growth_hbm, first_hbm, last_hbm, mass_out, fate_out,
    rows, cols, blocks, growth, labels, table, index, scaled, window, partial, edges, own_sum, fates,
    near_sum, far_sum, whole, message, messages,
    load_sem, block_sem, index_sem, send_sem, recv_sem, all_send_sem, all_recv_sem,
):
    tm, cell = lax.axis_index("tm"), lax.axis_index("cell")
    cells = lax.axis_size("cell")
    right, left = lax.rem(cell + 1, cells), lax.rem(cell + cells - 1, cells)
    slots, side, _ = blocks.shape
    dev_blocks = scaled.shape[0] - 1
    height = scaled.shape[1]
    per_row = slots // dev_blocks
    dev_cells = dev_blocks * side
    all_cells = dev_cells * cells
    reach = BAND_REACH
    steps = partial.shape[0]
    chunks = block_sem.shape[0]
    chunk = slots // chunks

    loads = [
        pltpu.make_async_copy(rows_hbm, rows, load_sem.at[0]),
        pltpu.make_async_copy(cols_hbm, cols, load_sem.at[1]),
        pltpu.make_async_copy(growth_hbm, growth, load_sem.at[2]),
    ]
    for load in loads:
        load.start()
    first_load = pltpu.make_async_copy(first_hbm, labels.at[1], load_sem.at[3])
    last_load = pltpu.make_async_copy(last_hbm, labels.at[1], load_sem.at[3])

    @pl.when(tm == 0)
    def _():
        first_load.start()

    @pl.when(tm == 1)
    def _():
        last_load.start()

    block_loads = [
        pltpu.make_async_copy(blocks_hbm.at[0, pl.ds(i * chunk, chunk)], blocks.at[pl.ds(i * chunk, chunk)], block_sem.at[i])
        for i in range(chunks)
    ]
    for load in block_loads:
        load.start()

    barrier = pltpu.get_barrier_semaphore()

    def greet(step, carry):
        pl.semaphore_signal(barrier, inc=1, device_id=(tm, lax.rem(cell + step, cells)), device_id_type=MESH)
        return carry

    for other in (left, cell, right):
        pl.semaphore_signal(barrier, inc=1, device_id=(1 - tm, other), device_id_type=MESH)
    lax.fori_loop(1, cells, greet, 0)

    loads[0].wait()
    loads[1].wait()
    make_tables(rows[...], cols[...], cell * dev_blocks, dev_blocks, per_row, steps, table)
    index_copy = pltpu.make_async_copy(table, index, index_sem)
    index_copy.start()
    loads[2].wait()
    last_load.wait()

    def remote(source, target, number, to_tm, to_cell):
        return pltpu.make_async_remote_copy(
            src_ref=source, dst_ref=target, send_sem=send_sem.at[number], recv_sem=recv_sem.at[number],
            device_id=(to_tm, to_cell), device_id_type=MESH,
        )

    def forward():
        total = None
        for step in range(steps):
            places = [step * GROUP + i for i in range(GROUP)]
            taken = jnp.concatenate([scaled[index[1, p]] for p in places], axis=1)
            stored = jnp.concatenate([blocks[index[0, p]] for p in places], axis=0)
            product = jnp.dot(taken, stored, preferred_element_type=F32)
            if step > 0:
                product = product + jnp.where(index[2, step] > 0, total, 0.0)
            total = product
            partial[step] = total

        def column(w):
            return jnp.where(index[4, w] > 0, partial[index[3, w]], 0.0)

        row_sum = None
        for w in range(dev_blocks + 2 * reach):
            value = column(w)
            row_sum = value if row_sum is None else row_sum + value
            if w < reach:
                edges[0, w] = value.astype(BF16)
            elif w < reach + dev_blocks:
                own_sum[w - reach] = value
            else:
                edges[1, w - reach - dev_blocks] = value.astype(BF16)
        return jnp.sum(row_sum.T, axis=0, keepdims=True)

    def backward(r):
        total = None
        for k in range(0, per_row, GROUP):
            places = [r * per_row + k + i for i in range(GROUP)]
            taken = jnp.concatenate([window[index[6, p]] for p in places], axis=1)
            stored = jnp.concatenate([blocks[index[5, p]] for p in places], axis=1)
            product = lax.dot_general(taken, stored, (((1,), (1,)), ((), ())), preferred_element_type=F32)
            total = product if total is None else total + product
        grouped = total.reshape(height // CELL_TYPES, CELL_TYPES, side)
        grouped = grouped * (CELL_TYPES / jnp.sum(grouped, axis=1, keepdims=True))
        return grouped.reshape(height, side).astype(BF16)

    def tell_all():
        def tell(step, carry):
            pltpu.make_async_remote_copy(
                src_ref=message, dst_ref=messages.at[cell], send_sem=all_send_sem, recv_sem=all_recv_sem,
                device_id=(tm, lax.rem(cell + step, cells)), device_id_type=MESH,
            ).start()
            return carry

        lax.fori_loop(1, cells, tell, 0)

    def hear_all():
        heard = pltpu.make_async_remote_copy(
            src_ref=messages.at[pl.ds(0, cells - 1)], dst_ref=messages.at[pl.ds(0, cells - 1)],
            send_sem=all_send_sem, recv_sem=all_recv_sem, device_id=(tm, right), device_id_type=MESH,
        )
        heard.wait()
        messages[cell] = message[...]
        sums, units = messages[:, 0, :], messages[:, 1, :]
        largest = jnp.max(units, axis=0, keepdims=True)
        total = jnp.sum(sums * (units / largest), axis=0, keepdims=True)
        factors = [all_cells * (messages[i][1:2] / largest) / total for i in (left, cell, right)]
        square = jnp.concatenate(factors + [jnp.zeros((height - 3, height), F32)], axis=0).T
        return [square[:, i : i + 1] for i in range(3)]

    def block_range(r):
        return pl.ds(r * side, side)

    @pl.when(tm == 0)
    def _():
        scaled[dev_blocks] = jnp.zeros((height, side), BF16)
        for r in range(dev_blocks):
            marks = one_hot(labels[1, :, block_range(r)])
            scaled[r] = (marks / growth[:, block_range(r)]).astype(BF16)
        index_copy.wait()
        for load in block_loads:
            load.wait()
        sums = forward()
        message[...] = jnp.concatenate([sums, jnp.ones_like(sums)], axis=0)
        pl.semaphore_wait(barrier, cells - 1 + 3)
        to_left = remote(edges.at[0], near_sum.at[1], 0, 1, left)
        to_right = remote(edges.at[1], near_sum.at[0], 1, 1, right)
        to_other = remote(own_sum, whole, 2, 1, cell)
        to_left.start()
        to_right.start()
        to_other.start()
        tell_all()
        remote(fates, window.at[pl.ds(0, reach)], 3, 1, left).wait_recv()
        remote(fates, window.at[pl.ds(reach, dev_blocks)], 4, 1, cell).wait_recv()
        remote(fates, window.at[pl.ds(reach + dev_blocks, reach)], 5, 1, right).wait_recv()
        for r in range(dev_blocks):
            fate_out[0, :, block_range(r)] = backward(r)
        remote(whole, whole, 6, 1, cell).wait_recv()
        factor = hear_all()[1]
        for r in range(dev_blocks):
            mass_out[0, :, block_range(r)] = (whole[r] * factor).astype(BF16)
        to_left.wait_send()
        to_right.wait_send()
        to_other.wait_send()

    @pl.when(tm == 1)
    def _():
        pl.semaphore_wait(barrier, cells - 1 + 3)
        labels_right = remote(labels.at[1], labels.at[0], 7, 1, right)
        labels_left = remote(labels.at[1], labels.at[2], 8, 1, left)
        labels_right.start()
        labels_left.start()
        for r in range(dev_blocks):
            window[reach + r] = one_hot(labels[1, :, block_range(r)]).astype(BF16)
        index_copy.wait()
        for load in block_loads:
            load.wait()
        labels_right.wait_recv()
        labels_left.wait_recv()
        for r in range(reach):
            window[r] = one_hot(labels[0, :, block_range(dev_blocks - reach + r)]).astype(BF16)
            window[reach + dev_blocks + r] = one_hot(labels[2, :, block_range(r)]).astype(BF16)
        for r in range(dev_blocks):
            value = backward(r)
            fates[r] = value
            fate_out[0, :, block_range(r)] = value
        fate_right = remote(fates, window.at[pl.ds(0, reach)], 3, 0, right)
        fate_here = remote(fates, window.at[pl.ds(reach, dev_blocks)], 4, 0, cell)
        fate_left = remote(fates, window.at[pl.ds(reach + dev_blocks, reach)], 5, 0, left)
        fate_right.start()
        fate_left.start()
        fate_here.start()

        remote(edges.at[0], near_sum.at[1], 0, 0, right).wait_recv()
        remote(edges.at[1], near_sum.at[0], 1, 0, left).wait_recv()
        remote(own_sum, whole, 2, 0, cell).wait_recv()
        row_sum = jnp.zeros((height, side), F32)
        for r in range(dev_blocks):
            value = whole[r] + near_sum[0, r].astype(F32) + near_sum[1, r].astype(F32)
            whole[r] = value
            row_sum = row_sum + value
        mass_back = remote(whole, whole, 6, 0, cell)
        mass_back.start()
        mean = jnp.sum(row_sum, axis=1, keepdims=True) * (1.0 / dev_cells)
        unit = jnp.where(mean > 0.0, mean, 1.0)
        unit = jnp.broadcast_to(unit, (height, side))
        scaled[dev_blocks] = jnp.zeros((height, side), BF16)
        for r in range(dev_blocks):
            scaled[r] = (whole[r] / unit / growth[:, block_range(r)]).astype(BF16)
        sums = forward()
        message[...] = jnp.concatenate([sums, unit.T[0:1]], axis=0)
        to_left = remote(edges.at[0], far_sum.at[1], 9, 1, left)
        to_right = remote(edges.at[1], far_sum.at[0], 10, 1, right)
        to_left.start()
        to_right.start()
        tell_all()
        to_left.wait_recv()
        to_right.wait_recv()
        factors = hear_all()
        for r in range(dev_blocks):
            value = own_sum[r] * factors[1] + far_sum[0, r].astype(F32) * factors[0] + far_sum[1, r].astype(F32) * factors[2]
            mass_out[0, :, block_range(r)] = value.astype(BF16)
        for copy in (labels_right, labels_left, fate_right, fate_here, fate_left, mass_back, to_left, to_right):
            copy.wait_send()


def on_device(block_rows, block_cols, block_values, growth, first_labels, last_labels):
    slots, side = block_values.shape[1], block_values.shape[2]
    dev_cells = growth.shape[1]
    dev_blocks = dev_cells // side
    panels = first_labels.shape[0]
    height = panels * CELL_TYPES
    cells = lax.axis_size("cell")
    columns = dev_blocks + 2 * BAND_REACH
    steps = (slots + (GROUP - 1) * columns) // GROUP
    out = jax.ShapeDtypeStruct((1, height, dev_cells), BF16)
    copies = 11
    return pl.pallas_call(
        kernel,
        out_shape=(out, out),
        in_specs=[pl.BlockSpec(memory_space=pl.ANY)] * 6,
        out_specs=(pl.BlockSpec(memory_space=pltpu.VMEM), pl.BlockSpec(memory_space=pltpu.VMEM)),
        scratch_shapes=[
            pltpu.VMEM((1, slots), jnp.int32),
            pltpu.VMEM((1, slots), jnp.int32),
            pltpu.VMEM((slots, side, side), BF16),
            pltpu.VMEM((1, dev_cells), F32),
            pltpu.VMEM((3, panels, dev_cells), jnp.int32),
            pltpu.VMEM((8, 128), jnp.int32),
            pltpu.SMEM((8, 128), jnp.int32),
            pltpu.VMEM((dev_blocks + 1, height, side), BF16),
            pltpu.VMEM((columns, height, side), BF16),
            pltpu.VMEM((steps, height, side), F32),
            pltpu.VMEM((2, BAND_REACH, height, side), BF16),
            pltpu.VMEM((dev_blocks, height, side), F32),
            pltpu.VMEM((dev_blocks, height, side), BF16),
            pltpu.VMEM((2, BAND_REACH, height, side), BF16),
            pltpu.VMEM((2, BAND_REACH, height, side), BF16),
            pltpu.VMEM((dev_blocks, height, side), F32),
            pltpu.VMEM((2, height), F32),
            pltpu.VMEM((cells, 2, height), F32),
            pltpu.SemaphoreType.DMA((4,)),
            pltpu.SemaphoreType.DMA((4,)),
            pltpu.SemaphoreType.DMA,
            pltpu.SemaphoreType.DMA((copies,)),
            pltpu.SemaphoreType.DMA((copies,)),
            pltpu.SemaphoreType.DMA,
            pltpu.SemaphoreType.DMA,
        ],
        compiler_params=pltpu.CompilerParams(collective_id=0, has_side_effects=True, vmem_limit_bytes=40 * 1024 * 1024),
    )(block_rows, block_cols, block_values, growth, first_labels, last_labels)


def solution(mesh):
    placed = (
        P("tm", "cell"),
        P("tm", "cell"),
        P("tm", "cell", None, None),
        P("tm", "cell"),
        P(None, "cell"),
        P(None, "cell"),
    )
    return jax.shard_map(
        on_device,
        mesh=mesh,
        in_specs=placed,
        out_specs=(P("tm", None, "cell"), P("tm", None, "cell")),
        check_vma=False,
    )
```

```python
import functools

import jax
import jax.numpy as jnp
from jax import lax
from jax.experimental import pallas as pl
from jax.experimental.pallas import tpu as pltpu
from jax.sharding import PartitionSpec as P

CELL_TYPES = 16
BAND_REACH = 4
GROUP = 4
MESH = pl.DeviceIdType.MESH
F32 = jnp.float32
BF16 = jnp.bfloat16


def make_tables(rows, cols, first_block, dev_blocks, per_row, steps, table):
    slots = rows.shape[1]
    lanes = table.shape[1]
    local_row = rows - first_block
    window_col = cols - first_block + BAND_REACH
    down = lax.broadcasted_iota(jnp.int32, (slots, slots), 0)
    across = lax.broadcasted_iota(jnp.int32, (slots, slots), 1)

    def upright(line):
        return jnp.sum(jnp.where(down == across, line, 0), axis=1, keepdims=True)

    row_of, col_of = upright(local_row), upright(window_col)
    earlier = across < down
    in_col = jnp.sum(jnp.where(earlier & (window_col == col_of), 1, 0), axis=1, keepdims=True)
    in_row = jnp.sum(jnp.where(earlier & (local_row == row_of), 1, 0), axis=1, keepdims=True)
    lane = lax.broadcasted_iota(jnp.int32, (slots, lanes), 1)
    slot = lax.broadcasted_iota(jnp.int32, (slots, lanes), 0)
    named = col_of == lane
    count = jnp.sum(jnp.where(named, 1, 0), axis=0, keepdims=True)
    groups = (count + (GROUP - 1)) // GROUP
    base = jnp.sum(jnp.where(lane < col_of, groups, 0), axis=1, keepdims=True)
    place = GROUP * base + in_col
    group_of = base + in_col // GROUP
    hit = place == lane
    group_hit = group_of == lane
    before_hit = group_of == lane - 1
    here = jnp.max(jnp.where(group_hit, col_of, -1), axis=0, keepdims=True)
    before = jnp.max(jnp.where(before_hit, col_of, -2), axis=0, keepdims=True)
    row_place = per_row * row_of + in_row
    row_hit = row_place == lane
    lines = (
        jnp.sum(jnp.where(hit, slot, 0), axis=0, keepdims=True),
        jnp.sum(jnp.where(hit, row_of - dev_blocks, 0), axis=0, keepdims=True) + dev_blocks,
        jnp.where(here == before, 1, 0),
        jnp.max(jnp.where(named, group_of, 0), axis=0, keepdims=True),
        jnp.where(count > 0, 1, 0),
        jnp.sum(jnp.where(row_hit, slot, 0), axis=0, keepdims=True),
        jnp.sum(jnp.where(row_hit, col_of, 0), axis=0, keepdims=True),
        jnp.zeros_like(count),
    )
    bounds = (slots - 1, dev_blocks, 1, steps - 1, 1, slots - 1, dev_blocks + 2 * BAND_REACH - 1, 0)
    lines = [jnp.clip(line, 0, bound) for line, bound in zip(lines, bounds)]
    table[...] = jnp.concatenate(lines, axis=0)


def one_hot(labels):
    panels, side = labels.shape
    kind = lax.broadcasted_iota(jnp.int32, (panels, CELL_TYPES, side), 1)
    marks = jnp.where(labels[:, None, :] == kind, 1.0, 0.0)
    return marks.reshape(panels * CELL_TYPES, side)


def kernel(
    rows_hbm, cols_hbm, blocks_hbm, growth_hbm, first_hbm, last_hbm, mass_out, fate_out,
    rows, cols, blocks, growth, labels, table, index, scaled, window, partial, edges, own_sum, fates,
    near_sum, far_sum, whole, first_total, first_factor, message, messages,
    load_sem, block_sem, index_sem, send_sem, recv_sem, all_send_sem, all_recv_sem,
):
    tm, cell = lax.axis_index("tm"), lax.axis_index("cell")
    cells = lax.axis_size("cell")
    right, left = lax.rem(cell + 1, cells), lax.rem(cell + cells - 1, cells)
    has_right, has_left = cell < cells - 1, cell > 0
    slots, side, _ = blocks.shape
    dev_blocks = scaled.shape[0] - 1
    height = scaled.shape[1]
    per_row = slots // dev_blocks
    dev_cells = dev_blocks * side
    all_cells = dev_cells * cells
    reach = BAND_REACH
    steps = partial.shape[0]
    chunks = block_sem.shape[0]
    chunk = slots // chunks

    load_rows = pltpu.make_async_copy(rows_hbm, rows, load_sem.at[0])
    load_cols = pltpu.make_async_copy(cols_hbm, cols, load_sem.at[1])
    load_growth = pltpu.make_async_copy(growth_hbm, growth, load_sem.at[2])
    load_first = pltpu.make_async_copy(first_hbm, labels.at[1], load_sem.at[3])
    load_last = pltpu.make_async_copy(last_hbm, labels.at[1], load_sem.at[3])
    load_passed = pltpu.make_async_copy(last_hbm, labels.at[0], load_sem.at[4])
    load_blocks = [
        pltpu.make_async_copy(blocks_hbm.at[0, pl.ds(i * chunk, chunk)], blocks.at[pl.ds(i * chunk, chunk)], block_sem.at[i])
        for i in range(chunks)
    ]
    barrier = pltpu.get_barrier_semaphore()

    def greet(to_tm, to_cell):
        pl.semaphore_signal(barrier, inc=1, device_id=(to_tm, to_cell), device_id_type=MESH)

    load_rows.start()
    load_cols.start()
    for load in load_blocks:
        load.start()
    load_growth.start()

    @pl.when(tm == 0)
    def _():
        load_first.start()
        load_passed.start()

    @pl.when(tm == 1)
    def _():
        load_last.start()
        greet(0, cell)

        @pl.when(has_left)
        def _():
            greet(0, left)

        @pl.when(has_right)
        def _():
            greet(0, right)

        def greet_all(step, carry):
            greet(1, lax.rem(cell + step, cells))
            return carry

        lax.fori_loop(1, cells, greet_all, 0)

    load_rows.wait()
    load_cols.wait()
    make_tables(rows[...], cols[...], cell * dev_blocks, dev_blocks, per_row, steps, table)
    index_copy = pltpu.make_async_copy(table, index, index_sem)
    index_copy.start()

    def remote(source, target, number, to_tm, to_cell):
        return pltpu.make_async_remote_copy(
            src_ref=source, dst_ref=target, send_sem=send_sem.at[number], recv_sem=recv_sem.at[number],
            device_id=(to_tm, to_cell), device_id_type=MESH,
        )

    def block_range(r):
        return pl.ds(r * side, side)

    def column_sums(beside=None):
        total = None
        for step in range(steps):
            places = [step * GROUP + i for i in range(GROUP)]
            taken = jnp.concatenate([scaled[index[1, p]] for p in places], axis=1)
            stored = jnp.concatenate([blocks[index[0, p]] for p in places], axis=0)
            product = jnp.dot(taken, stored, preferred_element_type=F32)
            if step > 0:
                product = product + jnp.where(index[2, step] > 0, total, 0.0)
            total = product
            partial[step] = total
            if beside is not None:
                beside(step)

    def column(w):
        return jnp.where(index[4, w] > 0, partial[index[3, w]], 0.0)

    def outer_columns():
        for w in range(reach):
            edges[0, w] = column(w).astype(BF16)
            edges[1, w] = column(reach + dev_blocks + w).astype(BF16)

    def own_columns():
        for w in range(dev_blocks):
            own_sum[w] = column(reach + w)

    def fate_block(r):
        total = None
        for k in range(0, per_row, GROUP):
            places = [r * per_row + k + i for i in range(GROUP)]
            taken = jnp.concatenate([window[index[6, p]] for p in places], axis=1)
            stored = jnp.concatenate([blocks[index[5, p]] for p in places], axis=1)
            product = lax.dot_general(taken, stored, (((1,), (1,)), ((), ())), preferred_element_type=F32)
            total = product if total is None else total + product
        grouped = total.reshape(height // CELL_TYPES, CELL_TYPES, side)
        grouped = grouped * (CELL_TYPES / jnp.sum(grouped, axis=1, keepdims=True))
        return grouped.reshape(height, side).astype(BF16)

    def row_totals(r):
        ones = jnp.ones((8, GROUP * side), BF16)
        total = None
        for k in range(0, per_row, GROUP):
            places = [r * per_row + k + i for i in range(GROUP)]
            stored = jnp.concatenate([blocks[index[5, p]] for p in places], axis=1)
            product = lax.dot_general(ones, stored, (((1,), (1,)), ((), ())), preferred_element_type=F32)
            total = product if total is None else total + product
        return total[0:1]

    @pl.when(tm == 0)
    def _():
        scaled[dev_blocks] = jnp.zeros((height, side), BF16)
        load_growth.wait()
        load_first.wait()
        for r in range(dev_blocks):
            marks = one_hot(labels[1, :, block_range(r)])
            scaled[r] = (marks / growth[:, block_range(r)]).astype(BF16)
        index_copy.wait()
        for load in load_blocks:
            load.wait()
        column_sums()
        outer_columns()
        load_passed.wait()
        labels_right = remote(labels.at[0], labels.at[0], 7, 1, right)
        labels_left = remote(labels.at[0], labels.at[2], 8, 1, left)
        edge_left = remote(edges.at[0], near_sum.at[1], 0, 1, left)
        edge_right = remote(edges.at[1], near_sum.at[0], 1, 1, right)
        own_here = remote(own_sum, whole, 2, 1, cell)
        total_here = remote(first_total, first_total, 11, 1, cell)
        pl.semaphore_wait(barrier, 2 + lax.div(cell + cells - 1, cells) - lax.div(cell + 1, cells))

        @pl.when(has_right)
        def _():
            edge_right.start()
            labels_right.start()

        @pl.when(has_left)
        def _():
            edge_left.start()
            labels_left.start()

        own_columns()
        own_here.start()
        row_sum = own_sum[0]
        for w in range(1, dev_blocks):
            row_sum = row_sum + own_sum[w]
        for w in range(reach):
            row_sum = row_sum + column(w) + column(reach + dev_blocks + w)
        first_total[...] = jnp.sum(row_sum.T, axis=0, keepdims=True)
        total_here.start()

        @pl.when(has_left)
        def _():
            remote(fates, window.at[pl.ds(0, reach)], 3, 1, left).wait_recv()

        @pl.when(has_right)
        def _():
            remote(fates, window.at[pl.ds(reach + dev_blocks, reach)], 5, 1, right).wait_recv()

        remote(fates, window.at[pl.ds(reach, dev_blocks)], 4, 1, cell).wait_recv()
        for r in range(dev_blocks):
            fate_out[0, :, block_range(r)] = fate_block(r)

        @pl.when(has_right)
        def _():
            edge_right.wait_send()
            labels_right.wait_send()

        @pl.when(has_left)
        def _():
            edge_left.wait_send()
            labels_left.wait_send()

        own_here.wait_send()
        total_here.wait_send()
        remote(whole, whole, 6, 1, cell).wait_recv()
        remote(first_factor, first_factor, 12, 1, cell).wait_recv()
        factor = jnp.broadcast_to(first_factor[...], (height, height)).T
        for r in range(dev_blocks):
            mass_out[0, :, block_range(r)] = (whole[r] * factor).astype(BF16)

    @pl.when(tm == 1)
    def _():
        load_last.wait()
        for r in range(dev_blocks):
            window[reach + r] = one_hot(labels[1, :, block_range(r)]).astype(BF16)
        index_copy.wait()
        for load in load_blocks:
            load.wait()
        totals = [row_totals(r) for r in range(dev_blocks)]
        scaled[dev_blocks] = jnp.zeros((height, side), BF16)
        load_growth.wait()

        @pl.when(has_left)
        def _():
            remote(labels.at[0], labels.at[0], 7, 0, left).wait_recv()
            for r in range(reach):
                window[r] = one_hot(labels[0, :, block_range(dev_blocks - reach + r)]).astype(BF16)

        @pl.when(has_right)
        def _():
            remote(labels.at[0], labels.at[2], 8, 0, right).wait_recv()
            for r in range(reach):
                window[reach + dev_blocks + r] = one_hot(labels[2, :, block_range(r)]).astype(BF16)

        for r in range(dev_blocks):
            value = fate_block(r)
            fates[r] = value
            fate_out[0, :, block_range(r)] = value
        remote(own_sum, whole, 2, 0, cell).wait_recv()
        fate_right = remote(fates, window.at[pl.ds(0, reach)], 3, 0, right)
        fate_here = remote(fates, window.at[pl.ds(reach, dev_blocks)], 4, 0, cell)
        fate_left = remote(fates, window.at[pl.ds(reach + dev_blocks, reach)], 5, 0, left)

        @pl.when(has_right)
        def _():
            fate_right.start()

        @pl.when(has_left)
        def _():
            fate_left.start()

        fate_here.start()

        @pl.when(has_right)
        def _():
            remote(edges.at[0], near_sum.at[1], 0, 0, right).wait_recv()

        @pl.when(has_left)
        def _():
            remote(edges.at[1], near_sum.at[0], 1, 0, left).wait_recv()

        @pl.when(jnp.logical_not(has_right))
        def _():
            near_sum[1] = jnp.zeros(near_sum.shape[1:], BF16)
            far_sum[1] = jnp.zeros(far_sum.shape[1:], BF16)

        @pl.when(jnp.logical_not(has_left))
        def _():
            near_sum[0] = jnp.zeros(near_sum.shape[1:], BF16)
            far_sum[0] = jnp.zeros(far_sum.shape[1:], BF16)

        row_sum = jnp.zeros((height, side), F32)
        for r in range(dev_blocks):
            value = whole[r] + near_sum[0, r].astype(F32) + near_sum[1, r].astype(F32)
            whole[r] = value
            row_sum = row_sum + value
        whole_back = remote(whole, whole, 6, 0, cell)
        whole_back.start()
        mean = jnp.sum(row_sum, axis=1, keepdims=True) * (1.0 / dev_cells)
        unit = jnp.broadcast_to(jnp.where(mean > 0.0, mean, 1.0), (height, side))
        weighted = jnp.zeros((height, side), F32)
        for r in range(dev_blocks):
            value = (whole[r] / unit / growth[:, block_range(r)]).astype(BF16)
            scaled[r] = value
            weighted = weighted + value.astype(F32) * totals[r]
        remote(first_total, first_total, 11, 0, cell).wait_recv()
        message[...] = jnp.concatenate([jnp.sum(weighted.T, axis=0, keepdims=True), unit.T[0:1], first_total[...], first_total[...]], axis=0)
        pl.semaphore_wait(barrier, cells - 1)

        def tell(step):
            pltpu.make_async_remote_copy(
                src_ref=message, dst_ref=messages.at[cell], send_sem=all_send_sem, recv_sem=all_recv_sem,
                device_id=(1, lax.rem(cell + step, cells)), device_id_type=MESH,
            ).start()

        share = -(-(cells - 1) // steps)

        def tell_some(step):
            for number in range(1 + step * share, min(1 + (step + 1) * share, cells)):
                tell(number)

        column_sums(tell_some)
        outer_columns()
        far_left = remote(edges.at[0], far_sum.at[1], 9, 1, left)
        far_right = remote(edges.at[1], far_sum.at[0], 10, 1, right)

        @pl.when(has_right)
        def _():
            far_right.start()

        @pl.when(has_left)
        def _():
            far_left.start()

        own_columns()
        heard = pltpu.make_async_remote_copy(
            src_ref=messages.at[pl.ds(0, cells - 1)], dst_ref=messages.at[pl.ds(0, cells - 1)],
            send_sem=all_send_sem, recv_sem=all_recv_sem, device_id=(1, lax.rem(cell + 1, cells)), device_id_type=MESH,
        )
        heard.wait()
        messages[cell] = message[...]
        first_factor[...] = all_cells / jnp.sum(messages[:, 2, :], axis=0, keepdims=True)
        factor_here = remote(first_factor, first_factor, 12, 0, cell)
        factor_here.start()
        sums, units = messages[:, 0, :], messages[:, 1, :]
        largest = jnp.max(units, axis=0, keepdims=True)
        total = jnp.sum(sums * (units / largest), axis=0, keepdims=True)
        sources = (left, cell, right)
        factors = [all_cells * (messages[i][1:2] / largest) / total for i in sources]
        square = jnp.concatenate(factors + [jnp.zeros((height - 3, height), F32)], axis=0).T
        factors = [square[:, i : i + 1] for i in range(3)]

        @pl.when(has_left)
        def _():
            remote(edges.at[1], far_sum.at[0], 10, 1, left).wait_recv()

        @pl.when(has_right)
        def _():
            remote(edges.at[0], far_sum.at[1], 9, 1, right).wait_recv()

        for r in range(dev_blocks):
            value = own_sum[r] * factors[1] + far_sum[0, r].astype(F32) * factors[0] + far_sum[1, r].astype(F32) * factors[2]
            mass_out[0, :, block_range(r)] = value.astype(BF16)

        @pl.when(has_right)
        def _():
            fate_right.wait_send()
            far_right.wait_send()

        @pl.when(has_left)
        def _():
            fate_left.wait_send()
            far_left.wait_send()

        fate_here.wait_send()
        whole_back.wait_send()
        factor_here.wait_send()


def on_device(block_rows, block_cols, block_values, growth, first_labels, last_labels):
    slots, side = block_values.shape[1], block_values.shape[2]
    dev_cells = growth.shape[1]
    dev_blocks = dev_cells // side
    panels = first_labels.shape[0]
    height = panels * CELL_TYPES
    cells = lax.axis_size("cell")
    columns = dev_blocks + 2 * BAND_REACH
    steps = (slots + (GROUP - 1) * columns) // GROUP
    out = jax.ShapeDtypeStruct((1, height, dev_cells), BF16)
    copies = 13
    return pl.pallas_call(
        kernel,
        out_shape=(out, out),
        in_specs=[pl.BlockSpec(memory_space=pl.ANY)] * 6,
        out_specs=(pl.BlockSpec(memory_space=pltpu.VMEM), pl.BlockSpec(memory_space=pltpu.VMEM)),
        scratch_shapes=[
            pltpu.VMEM((1, slots), jnp.int32),
            pltpu.VMEM((1, slots), jnp.int32),
            pltpu.VMEM((slots, side, side), BF16),
            pltpu.VMEM((1, dev_cells), F32),
            pltpu.VMEM((3, panels, dev_cells), jnp.int32),
            pltpu.VMEM((8, 128), jnp.int32),
            pltpu.SMEM((8, 128), jnp.int32),
            pltpu.VMEM((dev_blocks + 1, height, side), BF16),
            pltpu.VMEM((columns, height, side), BF16),
            pltpu.VMEM((steps, height, side), F32),
            pltpu.VMEM((2, BAND_REACH, height, side), BF16),
            pltpu.VMEM((dev_blocks, height, side), F32),
            pltpu.VMEM((dev_blocks, height, side), BF16),
            pltpu.VMEM((2, BAND_REACH, height, side), BF16),
            pltpu.VMEM((2, BAND_REACH, height, side), BF16),
            pltpu.VMEM((dev_blocks, height, side), F32),
            pltpu.VMEM((1, height), F32),
            pltpu.VMEM((1, height), F32),
            pltpu.VMEM((4, height), F32),
            pltpu.VMEM((cells, 4, height), F32),
            pltpu.SemaphoreType.DMA((5,)),
            pltpu.SemaphoreType.DMA((4,)),
            pltpu.SemaphoreType.DMA,
            pltpu.SemaphoreType.DMA((copies,)),
            pltpu.SemaphoreType.DMA((copies,)),
            pltpu.SemaphoreType.DMA,
            pltpu.SemaphoreType.DMA,
        ],
        compiler_params=pltpu.CompilerParams(collective_id=0, has_side_effects=True, vmem_limit_bytes=40 * 1024 * 1024),
    )(*[pltpu.with_memory_space_constraint(x, pltpu.HBM) for x in (block_rows, block_cols, block_values, growth, first_labels, last_labels)])


def solution(mesh):
    placed = (
        P("tm", "cell"),
        P("tm", "cell"),
        P("tm", "cell", None, None),
        P("tm", "cell"),
        P(None, "cell"),
        P(None, "cell"),
    )
    return jax.shard_map(
        on_device,
        mesh=mesh,
        in_specs=placed,
        out_specs=(P("tm", None, "cell"), P("tm", None, "cell")),
        check_vma=False,
    )
```

```python
import functools

import jax
import jax.numpy as jnp
from jax import lax
from jax.experimental import pallas as pl
from jax.experimental.pallas import tpu as pltpu
from jax.sharding import PartitionSpec as P

CELL_TYPES = 16
BAND_REACH = 4
GROUP = 4
MESH = pl.DeviceIdType.MESH
F32 = jnp.float32
BF16 = jnp.bfloat16


def make_tables(rows, cols, first_block, dev_blocks, per_row, steps, table):
    slots = rows.shape[1]
    lanes = table.shape[1]
    local_row = rows - first_block
    window_col = cols - first_block + BAND_REACH
    down = lax.broadcasted_iota(jnp.int32, (slots, slots), 0)
    across = lax.broadcasted_iota(jnp.int32, (slots, slots), 1)

    def upright(line):
        return jnp.sum(jnp.where(down == across, line, 0), axis=1, keepdims=True)

    row_of, col_of = upright(local_row), upright(window_col)
    earlier = across < down
    in_col = jnp.sum(jnp.where(earlier & (window_col == col_of), 1, 0), axis=1, keepdims=True)
    in_row = jnp.sum(jnp.where(earlier & (local_row == row_of), 1, 0), axis=1, keepdims=True)
    lane = lax.broadcasted_iota(jnp.int32, (slots, lanes), 1)
    slot = lax.broadcasted_iota(jnp.int32, (slots, lanes), 0)
    named = col_of == lane
    count = jnp.sum(jnp.where(named, 1, 0), axis=0, keepdims=True)
    groups = (count + (GROUP - 1)) // GROUP
    base = jnp.sum(jnp.where(lane < col_of, groups, 0), axis=1, keepdims=True)
    place = GROUP * base + in_col
    group_of = base + in_col // GROUP
    hit = place == lane
    group_hit = group_of == lane
    before_hit = group_of == lane - 1
    here = jnp.max(jnp.where(group_hit, col_of, -1), axis=0, keepdims=True)
    before = jnp.max(jnp.where(before_hit, col_of, -2), axis=0, keepdims=True)
    row_place = per_row * row_of + in_row
    row_hit = row_place == lane
    lines = (
        jnp.sum(jnp.where(hit, slot, 0), axis=0, keepdims=True),
        jnp.sum(jnp.where(hit, row_of - dev_blocks, 0), axis=0, keepdims=True) + dev_blocks,
        jnp.where(here == before, 1, 0),
        jnp.max(jnp.where(named, group_of, 0), axis=0, keepdims=True),
        jnp.where(count > 0, 1, 0),
        jnp.sum(jnp.where(row_hit, slot, 0), axis=0, keepdims=True),
        jnp.sum(jnp.where(row_hit, col_of, 0), axis=0, keepdims=True),
        jnp.zeros_like(count),
    )
    bounds = (slots - 1, dev_blocks, 1, steps - 1, 1, slots - 1, dev_blocks + 2 * BAND_REACH - 1, 0)
    lines = [jnp.clip(line, 0, bound) for line, bound in zip(lines, bounds)]
    table[...] = jnp.concatenate(lines, axis=0)


def one_hot(labels):
    panels, side = labels.shape
    kind = lax.broadcasted_iota(jnp.int32, (panels, CELL_TYPES, side), 1)
    marks = jnp.where(labels[:, None, :] == kind, 1.0, 0.0)
    return marks.reshape(panels * CELL_TYPES, side)


def kernel(
    rows_hbm, cols_hbm, blocks_hbm, growth_hbm, first_hbm, last_hbm, mass_out, fate_out,
    rows, cols, blocks, growth, per_growth, labels, table, index, scaled, window, partial, edges, own_sum, fates,
    near_sum, far_sum, whole, first_total, first_factor, message, messages,
    load_sem, block_sem, index_sem, send_sem, recv_sem, all_send_sem, all_recv_sem,
):
    tm, cell = lax.axis_index("tm"), lax.axis_index("cell")
    cells = lax.axis_size("cell")
    right, left = lax.rem(cell + 1, cells), lax.rem(cell + cells - 1, cells)
    has_right, has_left = cell < cells - 1, cell > 0
    slots, side, _ = blocks.shape
    dev_blocks = scaled.shape[0] - 1
    height = scaled.shape[1]
    per_row = slots // dev_blocks
    dev_cells = dev_blocks * side
    all_cells = dev_cells * cells
    reach = BAND_REACH
    steps = partial.shape[0]
    chunks = block_sem.shape[0]
    chunk = slots // chunks

    load_rows = pltpu.make_async_copy(rows_hbm, rows, load_sem.at[0])
    load_cols = pltpu.make_async_copy(cols_hbm, cols, load_sem.at[1])
    load_growth = pltpu.make_async_copy(growth_hbm, growth, load_sem.at[2])
    load_first = pltpu.make_async_copy(first_hbm, labels.at[1], load_sem.at[3])
    load_last = pltpu.make_async_copy(last_hbm, labels.at[1], load_sem.at[3])
    load_passed = pltpu.make_async_copy(last_hbm, labels.at[0], load_sem.at[4])
    load_blocks = [
        pltpu.make_async_copy(blocks_hbm.at[0, pl.ds(i * chunk, chunk)], blocks.at[pl.ds(i * chunk, chunk)], block_sem.at[i])
        for i in range(chunks)
    ]
    barrier = pltpu.get_barrier_semaphore()

    def greet(to_tm, to_cell):
        pl.semaphore_signal(barrier, inc=1, device_id=(to_tm, to_cell), device_id_type=MESH)

    load_rows.start()
    load_cols.start()

    @pl.when(tm == 1)
    def _():
        greet(0, cell)

        @pl.when(has_left)
        def _():
            greet(0, left)

        @pl.when(has_right)
        def _():
            greet(0, right)

    for load in load_blocks:
        load.start()
    load_growth.start()

    @pl.when(tm == 0)
    def _():
        load_first.start()
        load_passed.start()

    @pl.when(tm == 1)
    def _():
        load_last.start()

        def greet_all(step, carry):
            greet(1, lax.rem(cell + step, cells))
            return carry

        lax.fori_loop(1, cells, greet_all, 0)

    load_rows.wait()
    load_cols.wait()
    make_tables(rows[...], cols[...], cell * dev_blocks, dev_blocks, per_row, steps, table)
    index_copy = pltpu.make_async_copy(table, index, index_sem)
    index_copy.start()

    def remote(source, target, number, to_tm, to_cell):
        return pltpu.make_async_remote_copy(
            src_ref=source, dst_ref=target, send_sem=send_sem.at[number], recv_sem=recv_sem.at[number],
            device_id=(to_tm, to_cell), device_id_type=MESH,
        )

    def block_range(r):
        return pl.ds(r * side, side)

    def column_sums():
        total = None
        for step in range(steps):
            places = [step * GROUP + i for i in range(GROUP)]
            taken = jnp.concatenate([scaled[index[1, p]] for p in places], axis=1)
            stored = jnp.concatenate([blocks[index[0, p]] for p in places], axis=0)
            product = jnp.dot(taken, stored, preferred_element_type=F32)
            if step > 0:
                product = product + jnp.where(index[2, step] > 0, total, 0.0)
            total = product
            partial[step] = total

    def column(w):
        return jnp.where(index[4, w] > 0, partial[index[3, w]], 0.0)

    def outer_columns():
        for w in range(reach):
            edges[0, w] = column(w).astype(BF16)
            edges[1, w] = column(reach + dev_blocks + w).astype(BF16)

    def own_columns():
        for w in range(dev_blocks):
            own_sum[w] = column(reach + w)

    def fate_block(r):
        total = None
        for k in range(0, per_row, GROUP):
            places = [r * per_row + k + i for i in range(GROUP)]
            taken = jnp.concatenate([window[index[6, p]] for p in places], axis=1)
            stored = jnp.concatenate([blocks[index[5, p]] for p in places], axis=1)
            product = lax.dot_general(taken, stored, (((1,), (1,)), ((), ())), preferred_element_type=F32)
            total = product if total is None else total + product
        grouped = total.reshape(height // CELL_TYPES, CELL_TYPES, side)
        grouped = grouped * (CELL_TYPES / jnp.sum(grouped, axis=1, keepdims=True))
        return grouped.reshape(height, side).astype(BF16)

    def row_totals(r):
        ones = jnp.ones((8, GROUP * side), BF16)
        total = None
        for k in range(0, per_row, GROUP):
            places = [r * per_row + k + i for i in range(GROUP)]
            stored = jnp.concatenate([blocks[index[5, p]] for p in places], axis=1)
            product = lax.dot_general(ones, stored, (((1,), (1,)), ((), ())), preferred_element_type=F32)
            total = product if total is None else total + product
        return total[0:1]

    @pl.when(tm == 0)
    def _():
        scaled[dev_blocks] = jnp.zeros((height, side), BF16)
        load_growth.wait()
        load_first.wait()
        for r in range(dev_blocks):
            marks = one_hot(labels[1, :, block_range(r)])
            scaled[r] = (marks / growth[:, block_range(r)]).astype(BF16)
        index_copy.wait()
        for load in load_blocks:
            load.wait()
        column_sums()
        load_passed.wait()
        labels_right = remote(labels.at[0], labels.at[0], 7, 1, right)
        labels_left = remote(labels.at[0], labels.at[2], 8, 1, left)
        edge_left = remote(edges.at[0], near_sum.at[1], 0, 1, left)
        edge_right = remote(edges.at[1], near_sum.at[0], 1, 1, right)
        own_here = remote(own_sum, whole, 2, 1, cell)
        total_here = remote(first_total, first_total, 11, 1, cell)
        pl.semaphore_wait(barrier, 2 + lax.div(cell + cells - 1, cells) - lax.div(cell + 1, cells))

        @pl.when(has_right)
        def _():
            labels_right.start()

        @pl.when(has_left)
        def _():
            labels_left.start()

        outer_columns()

        @pl.when(has_right)
        def _():
            edge_right.start()

        @pl.when(has_left)
        def _():
            edge_left.start()

        own_columns()
        own_here.start()
        row_sum = own_sum[0]
        for w in range(1, dev_blocks):
            row_sum = row_sum + own_sum[w]
        for w in range(reach):
            row_sum = row_sum + column(w) + column(reach + dev_blocks + w)
        first_total[...] = jnp.sum(row_sum.T, axis=0, keepdims=True)
        total_here.start()

        @pl.when(has_left)
        def _():
            remote(fates, window.at[pl.ds(0, reach)], 3, 1, left).wait_recv()

        @pl.when(has_right)
        def _():
            remote(fates, window.at[pl.ds(reach + dev_blocks, reach)], 5, 1, right).wait_recv()

        remote(fates, window.at[pl.ds(reach, dev_blocks)], 4, 1, cell).wait_recv()
        for r in range(dev_blocks):
            fate_out[0, :, block_range(r)] = fate_block(r)

        @pl.when(has_right)
        def _():
            edge_right.wait_send()
            labels_right.wait_send()

        @pl.when(has_left)
        def _():
            edge_left.wait_send()
            labels_left.wait_send()

        own_here.wait_send()
        total_here.wait_send()
        remote(whole, whole, 6, 1, cell).wait_recv()
        remote(first_factor, first_factor, 12, 1, cell).wait_recv()
        factor = jnp.broadcast_to(first_factor[...], (height, height)).T
        for r in range(dev_blocks):
            mass_out[0, :, block_range(r)] = (whole[r] * factor).astype(BF16)

    @pl.when(tm == 1)
    def _():
        load_last.wait()
        for r in range(dev_blocks):
            window[reach + r] = one_hot(labels[1, :, block_range(r)]).astype(BF16)
        index_copy.wait()
        for load in load_blocks:
            load.wait()
        totals = [row_totals(r) for r in range(dev_blocks)]
        scaled[dev_blocks] = jnp.zeros((height, side), BF16)
        load_growth.wait()
        per_growth[...] = 1.0 / growth[...]

        @pl.when(has_left)
        def _():
            remote(labels.at[0], labels.at[0], 7, 0, left).wait_recv()
            for r in range(reach):
                window[r] = one_hot(labels[0, :, block_range(dev_blocks - reach + r)]).astype(BF16)

        @pl.when(has_right)
        def _():
            remote(labels.at[0], labels.at[2], 8, 0, right).wait_recv()
            for r in range(reach):
                window[reach + dev_blocks + r] = one_hot(labels[2, :, block_range(r)]).astype(BF16)

        for r in range(dev_blocks):
            value = fate_block(r)
            fates[r] = value
            fate_out[0, :, block_range(r)] = value
        remote(own_sum, whole, 2, 0, cell).wait_recv()
        fate_right = remote(fates, window.at[pl.ds(0, reach)], 3, 0, right)
        fate_here = remote(fates, window.at[pl.ds(reach, dev_blocks)], 4, 0, cell)
        fate_left = remote(fates, window.at[pl.ds(reach + dev_blocks, reach)], 5, 0, left)

        @pl.when(has_right)
        def _():
            fate_right.start()

        @pl.when(has_left)
        def _():
            fate_left.start()

        fate_here.start()

        @pl.when(has_right)
        def _():
            remote(edges.at[0], near_sum.at[1], 0, 0, right).wait_recv()

        @pl.when(has_left)
        def _():
            remote(edges.at[1], near_sum.at[0], 1, 0, left).wait_recv()

        @pl.when(jnp.logical_not(has_right))
        def _():
            near_sum[1] = jnp.zeros(near_sum.shape[1:], BF16)
            far_sum[1] = jnp.zeros(far_sum.shape[1:], BF16)

        @pl.when(jnp.logical_not(has_left))
        def _():
            near_sum[0] = jnp.zeros(near_sum.shape[1:], BF16)
            far_sum[0] = jnp.zeros(far_sum.shape[1:], BF16)

        row_sum = jnp.zeros((height, side), F32)
        for r in range(dev_blocks):
            value = whole[r] + near_sum[0, r].astype(F32) + near_sum[1, r].astype(F32)
            whole[r] = value
            row_sum = row_sum + value
        whole_back = remote(whole, whole, 6, 0, cell)
        whole_back.start()
        mean = jnp.sum(row_sum, axis=1, keepdims=True) * (1.0 / dev_cells)
        unit = jnp.where(mean > 0.0, mean, 1.0)
        per_unit = 1.0 / unit
        weighted = jnp.zeros((height, side), F32)
        for r in range(dev_blocks):
            value = (whole[r] * per_unit * per_growth[:, block_range(r)]).astype(BF16)
            scaled[r] = value
            weighted = weighted + value.astype(F32) * totals[r]
        remote(first_total, first_total, 11, 0, cell).wait_recv()
        message[:, 0:height] = jnp.sum(weighted.T, axis=0, keepdims=True)
        message[:, height : 2 * height] = jnp.broadcast_to(unit, (height, side)).T[0:1]
        message[:, 2 * height : 3 * height] = first_total[...]
        pl.semaphore_wait(barrier, cells - 1)

        def tell(step):
            pltpu.make_async_remote_copy(
                src_ref=message, dst_ref=messages.at[cell], send_sem=all_send_sem, recv_sem=all_recv_sem,
                device_id=(1, step + lax.div(step + cells - cell, cells)), device_id_type=MESH,
            ).start()

        for step in range(cells - 1):
            tell(step)
        column_sums()
        outer_columns()
        far_left = remote(edges.at[0], far_sum.at[1], 9, 1, left)
        far_right = remote(edges.at[1], far_sum.at[0], 10, 1, right)

        @pl.when(has_right)
        def _():
            far_right.start()

        @pl.when(has_left)
        def _():
            far_left.start()

        own_columns()
        heard = pltpu.make_async_remote_copy(
            src_ref=messages.at[pl.ds(0, cells - 1)], dst_ref=messages.at[pl.ds(0, cells - 1)],
            send_sem=all_send_sem, recv_sem=all_recv_sem, device_id=(1, lax.rem(cell + 1, cells)), device_id_type=MESH,
        )
        heard.wait()
        messages[cell] = message[...]
        first_factor[...] = all_cells / jnp.sum(messages[:, :, 2 * height : 3 * height], axis=0)
        factor_here = remote(first_factor, first_factor, 12, 0, cell)
        factor_here.start()
        sums, units = messages[:, :, 0:height], messages[:, :, height : 2 * height]
        per_largest = 1.0 / jnp.max(units, axis=0)
        common = all_cells / jnp.sum(sums * (units * per_largest), axis=0)
        factors = [messages[i][:, height : 2 * height] * per_largest * common for i in (left, cell, right)]
        square = jnp.concatenate(factors + [jnp.zeros((height - 3, height), F32)], axis=0).T
        factors = [square[:, i : i + 1] for i in range(3)]

        @pl.when(has_left)
        def _():
            remote(edges.at[1], far_sum.at[0], 10, 1, left).wait_recv()

        @pl.when(has_right)
        def _():
            remote(edges.at[0], far_sum.at[1], 9, 1, right).wait_recv()

        for r in range(dev_blocks):
            value = own_sum[r] * factors[1] + far_sum[0, r].astype(F32) * factors[0] + far_sum[1, r].astype(F32) * factors[2]
            mass_out[0, :, block_range(r)] = value.astype(BF16)

        @pl.when(has_right)
        def _():
            fate_right.wait_send()
            far_right.wait_send()

        @pl.when(has_left)
        def _():
            fate_left.wait_send()
            far_left.wait_send()

        fate_here.wait_send()
        whole_back.wait_send()
        factor_here.wait_send()


def hand_over(mass, fate, mass_out, fate_out, sems):
    copies = [pltpu.make_async_copy(mass, mass_out, sems.at[0]), pltpu.make_async_copy(fate, fate_out, sems.at[1])]
    for copy in copies:
        copy.start()
    for copy in copies:
        copy.wait()


def on_device(block_rows, block_cols, block_values, growth, first_labels, last_labels):
    slots, side = block_values.shape[1], block_values.shape[2]
    dev_cells = growth.shape[1]
    dev_blocks = dev_cells // side
    panels = first_labels.shape[0]
    height = panels * CELL_TYPES
    cells = lax.axis_size("cell")
    columns = dev_blocks + 2 * BAND_REACH
    steps = (slots + (GROUP - 1) * columns) // GROUP
    out = jax.ShapeDtypeStruct((1, height, dev_cells), BF16)
    copies = 13
    mass, fate = pl.pallas_call(
        kernel,
        out_shape=(out, out),
        in_specs=[pl.BlockSpec(memory_space=pl.ANY)] * 6,
        out_specs=(pl.BlockSpec(memory_space=pltpu.VMEM), pl.BlockSpec(memory_space=pltpu.VMEM)),
        scratch_shapes=[
            pltpu.VMEM((1, slots), jnp.int32),
            pltpu.VMEM((1, slots), jnp.int32),
            pltpu.VMEM((slots, side, side), BF16),
            pltpu.VMEM((1, dev_cells), F32),
            pltpu.VMEM((1, dev_cells), F32),
            pltpu.VMEM((3, panels, dev_cells), jnp.int32),
            pltpu.VMEM((8, 128), jnp.int32),
            pltpu.SMEM((8, 128), jnp.int32),
            pltpu.VMEM((dev_blocks + 1, height, side), BF16),
            pltpu.VMEM((columns, height, side), BF16),
            pltpu.VMEM((steps, height, side), F32),
            pltpu.VMEM((2, BAND_REACH, height, side), BF16),
            pltpu.VMEM((dev_blocks, height, side), F32),
            pltpu.VMEM((dev_blocks, height, side), BF16),
            pltpu.VMEM((2, BAND_REACH, height, side), BF16),
            pltpu.VMEM((2, BAND_REACH, height, side), BF16),
            pltpu.VMEM((dev_blocks, height, side), F32),
            pltpu.VMEM((1, height), F32),
            pltpu.VMEM((1, height), F32),
            pltpu.VMEM((1, 3 * height), F32),
            pltpu.VMEM((cells, 1, 3 * height), F32),
            pltpu.SemaphoreType.DMA((5,)),
            pltpu.SemaphoreType.DMA((4,)),
            pltpu.SemaphoreType.DMA,
            pltpu.SemaphoreType.DMA((copies,)),
            pltpu.SemaphoreType.DMA((copies,)),
            pltpu.SemaphoreType.DMA,
            pltpu.SemaphoreType.DMA,
        ],
        compiler_params=pltpu.CompilerParams(collective_id=0, has_side_effects=True, vmem_limit_bytes=40 * 1024 * 1024),
    )(*[pltpu.with_memory_space_constraint(x, pltpu.HBM) for x in (block_rows, block_cols, block_values, growth, first_labels, last_labels)])
    return pl.pallas_call(
        hand_over,
        out_shape=(out, out),
        in_specs=[pl.BlockSpec(memory_space=pl.ANY)] * 2,
        out_specs=(pl.BlockSpec(memory_space=pl.ANY), pl.BlockSpec(memory_space=pl.ANY)),
        scratch_shapes=[pltpu.SemaphoreType.DMA((2,))],
    )(pltpu.with_memory_space_constraint(mass, pltpu.VMEM), pltpu.with_memory_space_constraint(fate, pltpu.VMEM))


def solution(mesh):
    placed = (
        P("tm", "cell"),
        P("tm", "cell"),
        P("tm", "cell", None, None),
        P("tm", "cell"),
        P(None, "cell"),
        P(None, "cell"),
    )
    return jax.shard_map(
        on_device,
        mesh=mesh,
        in_specs=placed,
        out_specs=(P("tm", None, "cell"), P("tm", None, "cell")),
        check_vma=False,
    )
```

```python
import functools

import jax
import jax.numpy as jnp
from jax import lax
from jax.experimental import pallas as pl
from jax.experimental.pallas import tpu as pltpu
from jax.sharding import PartitionSpec as P

CELL_TYPES = 16
BAND_REACH = 4
GROUP = 2
JOIN = 8
MESH = pl.DeviceIdType.MESH
F32 = jnp.float32
BF16 = jnp.bfloat16


def make_tables(rows, cols, first_block, dev_blocks, per_row, steps, table):
    slots = rows.shape[1]
    lanes = table.shape[1]
    local_row = rows - first_block
    window_col = cols - first_block + BAND_REACH
    down = lax.broadcasted_iota(jnp.int32, (slots, slots), 0)
    across = lax.broadcasted_iota(jnp.int32, (slots, slots), 1)

    def upright(line):
        return jnp.sum(jnp.where(down == across, line, 0), axis=1, keepdims=True)

    row_of, col_of = upright(local_row), upright(window_col)
    earlier = across < down
    in_col = jnp.sum(jnp.where(earlier & (window_col == col_of), 1, 0), axis=1, keepdims=True)
    in_row = jnp.sum(jnp.where(earlier & (local_row == row_of), 1, 0), axis=1, keepdims=True)
    lane = lax.broadcasted_iota(jnp.int32, (slots, lanes), 1)
    slot = lax.broadcasted_iota(jnp.int32, (slots, lanes), 0)
    named = col_of == lane
    count = jnp.sum(jnp.where(named, 1, 0), axis=0, keepdims=True)
    groups = (count + (GROUP - 1)) // GROUP
    base = jnp.sum(jnp.where(lane < col_of, groups, 0), axis=1, keepdims=True)
    place = GROUP * base + in_col
    group_of = base + in_col // GROUP
    hit = place == lane
    group_hit = group_of == lane
    before_hit = group_of == lane - 1
    here = jnp.max(jnp.where(group_hit, col_of, -1), axis=0, keepdims=True)
    before = jnp.max(jnp.where(before_hit, col_of, -2), axis=0, keepdims=True)
    row_place = per_row * row_of + in_row
    row_hit = row_place == lane
    lines = (
        jnp.sum(jnp.where(hit, slot, 0), axis=0, keepdims=True),
        jnp.sum(jnp.where(hit, row_of - dev_blocks, 0), axis=0, keepdims=True) + dev_blocks,
        jnp.where(here == before, 1, 0),
        jnp.max(jnp.where(named, group_of, 0), axis=0, keepdims=True),
        jnp.where(count > 0, 1, 0),
        jnp.sum(jnp.where(row_hit, slot, 0), axis=0, keepdims=True),
        jnp.sum(jnp.where(row_hit, col_of, 0), axis=0, keepdims=True),
        jnp.zeros_like(count),
    )
    bounds = (slots - 1, dev_blocks, 1, steps - 1, 1, slots - 1, dev_blocks + 2 * BAND_REACH - 1, 0)
    lines = [jnp.clip(line, 0, bound) for line, bound in zip(lines, bounds)]
    table[...] = jnp.concatenate(lines, axis=0)


def one_hot(labels):
    panels, side = labels.shape
    kind = lax.broadcasted_iota(jnp.int32, (panels, CELL_TYPES, side), 1)
    marks = jnp.where(labels[:, None, :] == kind, 1.0, 0.0)
    return marks.reshape(panels * CELL_TYPES, side)


def kernel(
    rows_hbm, cols_hbm, blocks_hbm, growth_hbm, first_hbm, last_hbm, mass_out, fate_out,
    rows, cols, blocks, growth, per_growth, labels, table, index, scaled, window, partial, edges, own_sum, fates,
    near_sum, far_sum, whole, first_total, first_factor, message, messages,
    load_sem, block_sem, index_sem, send_sem, recv_sem, all_send_sem, all_recv_sem,
):
    tm, cell = lax.axis_index("tm"), lax.axis_index("cell")
    cells = lax.axis_size("cell")
    right, left = lax.rem(cell + 1, cells), lax.rem(cell + cells - 1, cells)
    has_right, has_left = cell < cells - 1, cell > 0
    slots, side, _ = blocks.shape
    dev_blocks = scaled.shape[0] - 1
    height = scaled.shape[1]
    per_row = slots // dev_blocks
    dev_cells = dev_blocks * side
    all_cells = dev_cells * cells
    reach = BAND_REACH
    steps = partial.shape[0]
    chunks = block_sem.shape[0]
    chunk = slots // chunks

    load_rows = pltpu.make_async_copy(rows_hbm, rows, load_sem.at[0])
    load_cols = pltpu.make_async_copy(cols_hbm, cols, load_sem.at[1])
    load_growth = pltpu.make_async_copy(growth_hbm, growth, load_sem.at[2])
    load_first = pltpu.make_async_copy(first_hbm, labels.at[1], load_sem.at[3])
    load_last = pltpu.make_async_copy(last_hbm, labels.at[1], load_sem.at[3])
    load_passed = pltpu.make_async_copy(last_hbm, labels.at[0], load_sem.at[4])
    load_blocks = [
        pltpu.make_async_copy(blocks_hbm.at[0, pl.ds(i * chunk, chunk)], blocks.at[pl.ds(i * chunk, chunk)], block_sem.at[i])
        for i in range(chunks)
    ]
    barrier = pltpu.get_barrier_semaphore()

    def greet(to_tm, to_cell):
        pl.semaphore_signal(barrier, inc=1, device_id=(to_tm, to_cell), device_id_type=MESH)

    load_rows.start()
    load_cols.start()

    @pl.when(tm == 1)
    def _():
        greet(0, cell)

        @pl.when(has_left)
        def _():
            greet(0, left)

        @pl.when(has_right)
        def _():
            greet(0, right)

    for load in load_blocks:
        load.start()
    load_growth.start()

    @pl.when(tm == 0)
    def _():
        load_first.start()
        load_passed.start()

    @pl.when(tm == 1)
    def _():
        load_last.start()

        def greet_all(step, carry):
            greet(1, lax.rem(cell + step, cells))
            return carry

        lax.fori_loop(1, cells, greet_all, 0)

    load_rows.wait()
    load_cols.wait()
    make_tables(rows[...], cols[...], cell * dev_blocks, dev_blocks, per_row, steps, table)
    index_copy = pltpu.make_async_copy(table, index, index_sem)
    index_copy.start()

    def remote(source, target, number, to_tm, to_cell):
        return pltpu.make_async_remote_copy(
            src_ref=source, dst_ref=target, send_sem=send_sem.at[number], recv_sem=recv_sem.at[number],
            device_id=(to_tm, to_cell), device_id_type=MESH,
        )

    def block_range(r):
        return pl.ds(r * side, side)

    def column_sums():
        total = None
        for step in range(steps):
            places = [step * GROUP + i for i in range(GROUP)]
            taken = jnp.concatenate([scaled[index[1, p]] for p in places], axis=1)
            stored = jnp.concatenate([blocks[index[0, p]] for p in places], axis=0)
            product = jnp.dot(taken, stored, preferred_element_type=F32)
            if step > 0:
                product = product + jnp.where(index[2, step] > 0, total, 0.0)
            total = product
            partial[step] = total

    def column(w):
        return jnp.where(index[4, w] > 0, partial[index[3, w]], 0.0)

    def outer_columns():
        for w in range(reach):
            edges[0, w] = column(w).astype(BF16)
            edges[1, w] = column(reach + dev_blocks + w).astype(BF16)

    def own_columns():
        for w in range(dev_blocks):
            own_sum[w] = column(reach + w)

    def fate_block(r):
        total = None
        for k in range(0, per_row, JOIN):
            places = [r * per_row + k + i for i in range(JOIN)]
            taken = jnp.concatenate([window[index[6, p]] for p in places], axis=1)
            stored = jnp.concatenate([blocks[index[5, p]] for p in places], axis=1)
            product = lax.dot_general(taken, stored, (((1,), (1,)), ((), ())), preferred_element_type=F32)
            total = product if total is None else total + product
        grouped = total.reshape(height // CELL_TYPES, CELL_TYPES, side)
        grouped = grouped * (CELL_TYPES / jnp.sum(grouped, axis=1, keepdims=True))
        return grouped.reshape(height, side).astype(BF16)

    def row_totals(r):
        ones = jnp.ones((8, JOIN * side), BF16)
        total = None
        for k in range(0, per_row, JOIN):
            places = [r * per_row + k + i for i in range(JOIN)]
            stored = jnp.concatenate([blocks[index[5, p]] for p in places], axis=1)
            product = lax.dot_general(ones, stored, (((1,), (1,)), ((), ())), preferred_element_type=F32)
            total = product if total is None else total + product
        return total[0:1]

    @pl.when(tm == 0)
    def _():
        scaled[dev_blocks] = jnp.zeros((height, side), BF16)
        load_growth.wait()
        load_first.wait()
        for r in range(dev_blocks):
            marks = one_hot(labels[1, :, block_range(r)])
            scaled[r] = (marks / growth[:, block_range(r)]).astype(BF16)
        index_copy.wait()
        for load in load_blocks:
            load.wait()
        column_sums()
        load_passed.wait()
        labels_right = remote(labels.at[0], labels.at[0], 7, 1, right)
        labels_left = remote(labels.at[0], labels.at[2], 8, 1, left)
        edge_left = remote(edges.at[0], near_sum.at[1], 0, 1, left)
        edge_right = remote(edges.at[1], near_sum.at[0], 1, 1, right)
        own_here = remote(own_sum, whole, 2, 1, cell)
        total_here = remote(first_total, first_total, 11, 1, cell)
        pl.semaphore_wait(barrier, 2 + lax.div(cell + cells - 1, cells) - lax.div(cell + 1, cells))

        @pl.when(has_right)
        def _():
            labels_right.start()

        @pl.when(has_left)
        def _():
            labels_left.start()

        outer_columns()

        @pl.when(has_right)
        def _():
            edge_right.start()

        @pl.when(has_left)
        def _():
            edge_left.start()

        own_columns()
        own_here.start()
        row_sum = own_sum[0]
        for w in range(1, dev_blocks):
            row_sum = row_sum + own_sum[w]
        for w in range(reach):
            row_sum = row_sum + column(w) + column(reach + dev_blocks + w)
        first_total[...] = jnp.sum(row_sum.T, axis=0, keepdims=True)
        total_here.start()

        @pl.when(has_left)
        def _():
            remote(fates, window.at[pl.ds(0, reach)], 3, 1, left).wait_recv()

        @pl.when(has_right)
        def _():
            remote(fates, window.at[pl.ds(reach + dev_blocks, reach)], 5, 1, right).wait_recv()

        remote(fates, window.at[pl.ds(reach, dev_blocks)], 4, 1, cell).wait_recv()
        for r in range(dev_blocks):
            fate_out[0, :, block_range(r)] = fate_block(r)

        @pl.when(has_right)
        def _():
            edge_right.wait_send()
            labels_right.wait_send()

        @pl.when(has_left)
        def _():
            edge_left.wait_send()
            labels_left.wait_send()

        own_here.wait_send()
        total_here.wait_send()
        remote(whole, whole, 6, 1, cell).wait_recv()
        remote(first_factor, first_factor, 12, 1, cell).wait_recv()
        factor = jnp.broadcast_to(first_factor[...], (height, height)).T
        for r in range(dev_blocks):
            mass_out[0, :, block_range(r)] = (whole[r] * factor).astype(BF16)

    @pl.when(tm == 1)
    def _():
        load_last.wait()
        for r in range(dev_blocks):
            window[reach + r] = one_hot(labels[1, :, block_range(r)]).astype(BF16)
        index_copy.wait()
        for load in load_blocks:
            load.wait()
        totals = [row_totals(r) for r in range(dev_blocks)]
        scaled[dev_blocks] = jnp.zeros((height, side), BF16)
        load_growth.wait()
        per_growth[...] = 1.0 / growth[...]

        @pl.when(has_left)
        def _():
            remote(labels.at[0], labels.at[0], 7, 0, left).wait_recv()
            for r in range(reach):
                window[r] = one_hot(labels[0, :, block_range(dev_blocks - reach + r)]).astype(BF16)

        @pl.when(has_right)
        def _():
            remote(labels.at[0], labels.at[2], 8, 0, right).wait_recv()
            for r in range(reach):
                window[reach + dev_blocks + r] = one_hot(labels[2, :, block_range(r)]).astype(BF16)

        for r in range(dev_blocks):
            value = fate_block(r)
            fates[r] = value
            fate_out[0, :, block_range(r)] = value
        remote(own_sum, whole, 2, 0, cell).wait_recv()
        fate_right = remote(fates, window.at[pl.ds(0, reach)], 3, 0, right)
        fate_here = remote(fates, window.at[pl.ds(reach, dev_blocks)], 4, 0, cell)
        fate_left = remote(fates, window.at[pl.ds(reach + dev_blocks, reach)], 5, 0, left)


        @pl.when(has_right)
        def _():
            remote(edges.at[0], near_sum.at[1], 0, 0, right).wait_recv()

        @pl.when(has_left)
        def _():
            remote(edges.at[1], near_sum.at[0], 1, 0, left).wait_recv()

        @pl.when(jnp.logical_not(has_right))
        def _():
            near_sum[1] = jnp.zeros(near_sum.shape[1:], BF16)
            far_sum[1] = jnp.zeros(far_sum.shape[1:], BF16)

        @pl.when(jnp.logical_not(has_left))
        def _():
            near_sum[0] = jnp.zeros(near_sum.shape[1:], BF16)
            far_sum[0] = jnp.zeros(far_sum.shape[1:], BF16)

        row_sum = jnp.zeros((height, side), F32)
        for r in range(dev_blocks):
            value = whole[r] + near_sum[0, r].astype(F32) + near_sum[1, r].astype(F32)
            whole[r] = value
            row_sum = row_sum + value
        whole_back = remote(whole, whole, 6, 0, cell)
        mean = jnp.sum(row_sum, axis=1, keepdims=True) * (1.0 / dev_cells)
        unit = jnp.where(mean > 0.0, mean, 1.0)
        per_unit = 1.0 / unit
        weighted = jnp.zeros((height, side), F32)
        for r in range(dev_blocks):
            value = (whole[r] * per_unit * per_growth[:, block_range(r)]).astype(BF16)
            scaled[r] = value
            weighted = weighted + value.astype(F32) * totals[r]
        remote(first_total, first_total, 11, 0, cell).wait_recv()
        message[:, 0:height] = jnp.sum(weighted.T, axis=0, keepdims=True)
        message[:, height : 2 * height] = jnp.broadcast_to(unit, (height, side)).T[0:1]
        message[:, 2 * height : 3 * height] = first_total[...]
        pl.semaphore_wait(barrier, cells - 1)

        def tell(step):
            pltpu.make_async_remote_copy(
                src_ref=message, dst_ref=messages.at[cell], send_sem=all_send_sem, recv_sem=all_recv_sem,
                device_id=(1, step + lax.div(step + cells - cell, cells)), device_id_type=MESH,
            ).start()

        for step in range(cells - 1):
            tell(step)
        @pl.when(has_right)
        def _():
            fate_right.start()

        @pl.when(has_left)
        def _():
            fate_left.start()

        fate_here.start()
        whole_back.start()
        column_sums()
        outer_columns()
        far_left = remote(edges.at[0], far_sum.at[1], 9, 1, left)
        far_right = remote(edges.at[1], far_sum.at[0], 10, 1, right)

        @pl.when(has_right)
        def _():
            far_right.start()

        @pl.when(has_left)
        def _():
            far_left.start()

        own_columns()
        heard = pltpu.make_async_remote_copy(
            src_ref=messages.at[pl.ds(0, cells - 1)], dst_ref=messages.at[pl.ds(0, cells - 1)],
            send_sem=all_send_sem, recv_sem=all_recv_sem, device_id=(1, lax.rem(cell + 1, cells)), device_id_type=MESH,
        )
        heard.wait()
        messages[cell] = message[...]
        first_factor[...] = all_cells / jnp.sum(messages[:, :, 2 * height : 3 * height], axis=0)
        factor_here = remote(first_factor, first_factor, 12, 0, cell)
        factor_here.start()
        sums, units = messages[:, :, 0:height], messages[:, :, height : 2 * height]
        per_largest = 1.0 / jnp.max(units, axis=0)
        common = all_cells / jnp.sum(sums * (units * per_largest), axis=0)
        factors = [messages[i][:, height : 2 * height] * per_largest * common for i in (left, cell, right)]
        square = jnp.concatenate(factors + [jnp.zeros((height - 3, height), F32)], axis=0).T
        factors = [square[:, i : i + 1] for i in range(3)]

        @pl.when(has_left)
        def _():
            remote(edges.at[1], far_sum.at[0], 10, 1, left).wait_recv()

        @pl.when(has_right)
        def _():
            remote(edges.at[0], far_sum.at[1], 9, 1, right).wait_recv()

        for r in range(dev_blocks):
            value = own_sum[r] * factors[1] + far_sum[0, r].astype(F32) * factors[0] + far_sum[1, r].astype(F32) * factors[2]
            mass_out[0, :, block_range(r)] = value.astype(BF16)

        @pl.when(has_right)
        def _():
            fate_right.wait_send()
            far_right.wait_send()

        @pl.when(has_left)
        def _():
            fate_left.wait_send()
            far_left.wait_send()

        fate_here.wait_send()
        whole_back.wait_send()
        factor_here.wait_send()


def hand_over(mass, fate, mass_out, fate_out, sems):
    copies = [pltpu.make_async_copy(mass, mass_out, sems.at[0]), pltpu.make_async_copy(fate, fate_out, sems.at[1])]
    for copy in copies:
        copy.start()
    for copy in copies:
        copy.wait()


def on_device(block_rows, block_cols, block_values, growth, first_labels, last_labels):
    slots, side = block_values.shape[1], block_values.shape[2]
    dev_cells = growth.shape[1]
    dev_blocks = dev_cells // side
    panels = first_labels.shape[0]
    height = panels * CELL_TYPES
    cells = lax.axis_size("cell")
    columns = dev_blocks + 2 * BAND_REACH
    steps = (slots + (GROUP - 1) * columns) // GROUP
    out = jax.ShapeDtypeStruct((1, height, dev_cells), BF16)
    copies = 13
    mass, fate = pl.pallas_call(
        kernel,
        out_shape=(out, out),
        in_specs=[pl.BlockSpec(memory_space=pl.ANY)] * 6,
        out_specs=(pl.BlockSpec(memory_space=pltpu.VMEM), pl.BlockSpec(memory_space=pltpu.VMEM)),
        scratch_shapes=[
            pltpu.VMEM((1, slots), jnp.int32),
            pltpu.VMEM((1, slots), jnp.int32),
            pltpu.VMEM((slots, side, side), BF16),
            pltpu.VMEM((1, dev_cells), F32),
            pltpu.VMEM((1, dev_cells), F32),
            pltpu.VMEM((3, panels, dev_cells), jnp.int32),
            pltpu.VMEM((8, 128), jnp.int32),
            pltpu.SMEM((8, 128), jnp.int32),
            pltpu.VMEM((dev_blocks + 1, height, side), BF16),
            pltpu.VMEM((columns, height, side), BF16),
            pltpu.VMEM((steps, height, side), F32),
            pltpu.VMEM((2, BAND_REACH, height, side), BF16),
            pltpu.VMEM((dev_blocks, height, side), F32),
            pltpu.VMEM((dev_blocks, height, side), BF16),
            pltpu.VMEM((2, BAND_REACH, height, side), BF16),
            pltpu.VMEM((2, BAND_REACH, height, side), BF16),
            pltpu.VMEM((dev_blocks, height, side), F32),
            pltpu.VMEM((1, height), F32),
            pltpu.VMEM((1, height), F32),
            pltpu.VMEM((1, 3 * height), F32),
            pltpu.VMEM((cells, 1, 3 * height), F32),
            pltpu.SemaphoreType.DMA((5,)),
            pltpu.SemaphoreType.DMA((4,)),
            pltpu.SemaphoreType.DMA,
            pltpu.SemaphoreType.DMA((copies,)),
            pltpu.SemaphoreType.DMA((copies,)),
            pltpu.SemaphoreType.DMA,
            pltpu.SemaphoreType.DMA,
        ],
        compiler_params=pltpu.CompilerParams(collective_id=0, has_side_effects=True, vmem_limit_bytes=40 * 1024 * 1024),
    )(*[pltpu.with_memory_space_constraint(x, pltpu.HBM) for x in (block_rows, block_cols, block_values, growth, first_labels, last_labels)])
    return pl.pallas_call(
        hand_over,
        out_shape=(out, out),
        in_specs=[pl.BlockSpec(memory_space=pl.ANY)] * 2,
        out_specs=(pl.BlockSpec(memory_space=pl.ANY), pl.BlockSpec(memory_space=pl.ANY)),
        scratch_shapes=[pltpu.SemaphoreType.DMA((2,))],
    )(pltpu.with_memory_space_constraint(mass, pltpu.VMEM), pltpu.with_memory_space_constraint(fate, pltpu.VMEM))


def solution(mesh):
    placed = (
        P("tm", "cell"),
        P("tm", "cell"),
        P("tm", "cell", None, None),
        P("tm", "cell"),
        P(None, "cell"),
        P(None, "cell"),
    )
    return jax.shard_map(
        on_device,
        mesh=mesh,
        in_specs=placed,
        out_specs=(P("tm", None, "cell"), P("tm", None, "cell")),
        check_vma=False,
    )
```

```python
import functools

import jax
import jax.numpy as jnp
from jax import lax
from jax.experimental import pallas as pl
from jax.experimental.pallas import tpu as pltpu
from jax.sharding import PartitionSpec as P

CELL_TYPES = 16
BAND_REACH = 4
GROUP = 2
JOIN = 8
MESH = pl.DeviceIdType.MESH
F32 = jnp.float32
BF16 = jnp.bfloat16


def make_tables(rows, cols, first_block, dev_blocks, per_row, steps, table):
    slots = rows.shape[1]
    lanes = table.shape[1]
    local_row = rows - first_block
    window_col = cols - first_block + BAND_REACH
    down = lax.broadcasted_iota(jnp.int32, (slots, slots), 0)
    across = lax.broadcasted_iota(jnp.int32, (slots, slots), 1)

    def upright(line):
        return jnp.sum(jnp.where(down == across, line, 0), axis=1, keepdims=True)

    row_of, col_of = upright(local_row), upright(window_col)
    earlier = across < down
    in_col = jnp.sum(jnp.where(earlier & (window_col == col_of), 1, 0), axis=1, keepdims=True)
    in_row = jnp.sum(jnp.where(earlier & (local_row == row_of), 1, 0), axis=1, keepdims=True)
    lane = lax.broadcasted_iota(jnp.int32, (slots, lanes), 1)
    slot = lax.broadcasted_iota(jnp.int32, (slots, lanes), 0)
    named = col_of == lane
    count = jnp.sum(jnp.where(named, 1, 0), axis=0, keepdims=True)
    groups = (count + (GROUP - 1)) // GROUP
    base = jnp.sum(jnp.where(lane < col_of, groups, 0), axis=1, keepdims=True)
    place = GROUP * base + in_col
    group_of = base + in_col // GROUP
    hit = place == lane
    group_hit = group_of == lane
    before_hit = group_of == lane - 1
    here = jnp.max(jnp.where(group_hit, col_of, -1), axis=0, keepdims=True)
    before = jnp.max(jnp.where(before_hit, col_of, -2), axis=0, keepdims=True)
    row_place = per_row * row_of + in_row
    row_hit = row_place == lane
    lines = (
        jnp.sum(jnp.where(hit, slot, 0), axis=0, keepdims=True),
        jnp.sum(jnp.where(hit, row_of - dev_blocks, 0), axis=0, keepdims=True) + dev_blocks,
        jnp.where(here == before, 1, 0),
        jnp.max(jnp.where(named, group_of, 0), axis=0, keepdims=True),
        jnp.where(count > 0, 1, 0),
        jnp.sum(jnp.where(row_hit, slot, 0), axis=0, keepdims=True),
        jnp.sum(jnp.where(row_hit, col_of, 0), axis=0, keepdims=True),
        jnp.zeros_like(count),
    )
    bounds = (slots - 1, dev_blocks, 1, steps - 1, 1, slots - 1, dev_blocks + 2 * BAND_REACH - 1, 0)
    lines = [jnp.clip(line, 0, bound) for line, bound in zip(lines, bounds)]
    table[...] = jnp.concatenate(lines, axis=0)


def one_hot(labels):
    panels, side = labels.shape
    kind = lax.broadcasted_iota(jnp.int32, (panels, CELL_TYPES, side), 1)
    marks = jnp.where(labels[:, None, :] == kind, 1.0, 0.0)
    return marks.reshape(panels * CELL_TYPES, side)


def kernel(
    rows_hbm, cols_hbm, blocks_hbm, growth_hbm, first_hbm, last_hbm, mass_out, fate_out,
    rows, cols, blocks, growth, per_growth, labels, table, index, scaled, window, partial, edges, own_sum, fates,
    near_sum, far_sum, spare, whole, weights, weights_left, far_unit, first_total, first_factor, message, messages,
    load_sem, block_sem, index_sem, send_sem, recv_sem, all_send_sem, all_recv_sem,
):
    tm, cell = lax.axis_index("tm"), lax.axis_index("cell")
    cells = lax.axis_size("cell")
    right, left = lax.rem(cell + 1, cells), lax.rem(cell + cells - 1, cells)
    has_right, has_left = cell < cells - 1, cell > 0
    slots, side, _ = blocks.shape
    dev_blocks = scaled.shape[0] - 1
    height = scaled.shape[1]
    per_row = slots // dev_blocks
    dev_cells = dev_blocks * side
    all_cells = dev_cells * cells
    reach = BAND_REACH
    steps = partial.shape[0]
    chunks = block_sem.shape[0]
    chunk = slots // chunks

    load_rows = pltpu.make_async_copy(rows_hbm, rows, load_sem.at[0])
    load_cols = pltpu.make_async_copy(cols_hbm, cols, load_sem.at[1])
    load_growth = pltpu.make_async_copy(growth_hbm, growth, load_sem.at[2])
    load_first = pltpu.make_async_copy(first_hbm, labels.at[1], load_sem.at[3])
    load_last = pltpu.make_async_copy(last_hbm, labels.at[1], load_sem.at[3])
    load_passed = pltpu.make_async_copy(last_hbm, labels.at[0], load_sem.at[4])
    load_blocks = [
        pltpu.make_async_copy(blocks_hbm.at[0, pl.ds(i * chunk, chunk)], blocks.at[pl.ds(i * chunk, chunk)], block_sem.at[i])
        for i in range(chunks)
    ]
    barrier = pltpu.get_barrier_semaphore()

    def greet(to_tm, to_cell):
        pl.semaphore_signal(barrier, inc=1, device_id=(to_tm, to_cell), device_id_type=MESH)

    load_rows.start()
    load_cols.start()

    @pl.when(tm == 1)
    def _():
        greet(0, cell)

        @pl.when(has_left)
        def _():
            greet(0, left)

        @pl.when(has_right)
        def _():
            greet(0, right)

    for load in load_blocks:
        load.start()
    load_growth.start()

    @pl.when(tm == 0)
    def _():
        load_first.start()
        load_passed.start()

    @pl.when(tm == 1)
    def _():
        load_last.start()

        def greet_all(step, carry):
            greet(1, lax.rem(cell + step, cells))
            return carry

        lax.fori_loop(1, cells, greet_all, 0)

    load_rows.wait()
    load_cols.wait()
    make_tables(rows[...], cols[...], cell * dev_blocks, dev_blocks, per_row, steps, table)
    index_copy = pltpu.make_async_copy(table, index, index_sem)
    index_copy.start()

    def remote(source, target, number, to_tm, to_cell):
        return pltpu.make_async_remote_copy(
            src_ref=source, dst_ref=target, send_sem=send_sem.at[number], recv_sem=recv_sem.at[number],
            device_id=(to_tm, to_cell), device_id_type=MESH,
        )

    def block_range(r):
        return pl.ds(r * side, side)

    def column_sums():
        total = None
        for step in range(steps):
            places = [step * GROUP + i for i in range(GROUP)]
            taken = jnp.concatenate([scaled[index[1, p]] for p in places], axis=1)
            stored = jnp.concatenate([blocks[index[0, p]] for p in places], axis=0)
            product = jnp.dot(taken, stored, preferred_element_type=F32)
            if step > 0:
                product = product + jnp.where(index[2, step] > 0, total, 0.0)
            total = product
            partial[step] = total

    def column(w):
        return jnp.where(index[4, w] > 0, partial[index[3, w]], 0.0)

    def outer_columns():
        for w in range(reach):
            edges[0, w] = column(w).astype(BF16)
            edges[1, w] = column(reach + dev_blocks + w).astype(BF16)

    def own_columns():
        for w in range(dev_blocks):
            own_sum[w] = column(reach + w)

    def fate_block(r):
        total = None
        for k in range(0, per_row, JOIN):
            places = [r * per_row + k + i for i in range(JOIN)]
            taken = jnp.concatenate([window[index[6, p]] for p in places], axis=1)
            stored = jnp.concatenate([blocks[index[5, p]] for p in places], axis=1)
            product = lax.dot_general(taken, stored, (((1,), (1,)), ((), ())), preferred_element_type=F32)
            total = product if total is None else total + product
        grouped = total.reshape(height // CELL_TYPES, CELL_TYPES, side)
        grouped = grouped * (CELL_TYPES / jnp.sum(grouped, axis=1, keepdims=True))
        return grouped.reshape(height, side).astype(BF16)

    def row_totals(r):
        ones = jnp.ones((8, JOIN * side), BF16)
        total = None
        for k in range(0, per_row, JOIN):
            places = [r * per_row + k + i for i in range(JOIN)]
            stored = jnp.concatenate([blocks[index[5, p]] for p in places], axis=1)
            product = lax.dot_general(ones, stored, (((1,), (1,)), ((), ())), preferred_element_type=F32)
            total = product if total is None else total + product
        return total[0:1]

    @pl.when(tm == 0)
    def _():
        scaled[dev_blocks] = jnp.zeros((height, side), BF16)
        load_growth.wait()
        load_first.wait()
        for r in range(dev_blocks):
            marks = one_hot(labels[1, :, block_range(r)])
            scaled[r] = (marks / growth[:, block_range(r)]).astype(BF16)
        index_copy.wait()
        for load in load_blocks:
            load.wait()
        column_sums()
        load_passed.wait()
        labels_right = remote(labels.at[0], labels.at[0], 7, 1, right)
        labels_left = remote(labels.at[0], labels.at[2], 8, 1, left)
        edge_left = remote(edges.at[0], near_sum.at[1], 0, 1, left)
        edge_right = remote(edges.at[1], near_sum.at[0], 1, 1, right)
        own_here = remote(own_sum, whole, 2, 1, cell)
        spare_here = remote(edges.at[0], spare, 13, 1, cell)
        total_here = remote(first_total, first_total, 11, 1, cell)
        pl.semaphore_wait(barrier, 2 + lax.div(cell + cells - 1, cells) - lax.div(cell + 1, cells))

        @pl.when(has_right)
        def _():
            labels_right.start()

        @pl.when(has_left)
        def _():
            labels_left.start()

        outer_columns()

        @pl.when(has_right)
        def _():
            edge_right.start()

        @pl.when(has_left)
        def _():
            edge_left.start()
            spare_here.start()

        own_columns()
        own_here.start()
        row_sum = own_sum[0]
        for w in range(1, dev_blocks):
            row_sum = row_sum + own_sum[w]
        for w in range(reach):
            row_sum = row_sum + column(w) + column(reach + dev_blocks + w)
        first_total[...] = jnp.sum(row_sum.T, axis=0, keepdims=True)
        total_here.start()

        @pl.when(has_left)
        def _():
            remote(fates, window.at[pl.ds(0, reach)], 3, 1, left).wait_recv()

        @pl.when(has_right)
        def _():
            remote(fates, window.at[pl.ds(reach + dev_blocks, reach)], 5, 1, right).wait_recv()

        remote(fates, window.at[pl.ds(reach, dev_blocks)], 4, 1, cell).wait_recv()
        for r in range(dev_blocks):
            fate_out[0, :, block_range(r)] = fate_block(r)

        @pl.when(has_right)
        def _():
            edge_right.wait_send()
            labels_right.wait_send()

        @pl.when(has_left)
        def _():
            edge_left.wait_send()
            labels_left.wait_send()
            spare_here.wait_send()

        own_here.wait_send()
        total_here.wait_send()
        remote(whole, whole, 6, 1, cell).wait_recv()
        remote(first_factor, first_factor, 12, 1, cell).wait_recv()
        factor = jnp.broadcast_to(first_factor[...], (height, height)).T
        for r in range(dev_blocks):
            mass_out[0, :, block_range(r)] = (whole[r] * factor).astype(BF16)

    @pl.when(tm == 1)
    def _():
        load_last.wait()
        for r in range(dev_blocks):
            window[reach + r] = one_hot(labels[1, :, block_range(r)]).astype(BF16)
        index_copy.wait()
        for load in load_blocks:
            load.wait()
        totals = [row_totals(r) for r in range(dev_blocks)]
        scaled[dev_blocks] = jnp.zeros((height, side), BF16)
        load_growth.wait()
        per_growth[...] = 1.0 / growth[...]
        for r in range(dev_blocks):
            weights[:, block_range(r)] = totals[r] * per_growth[:, block_range(r)]
        pl.semaphore_wait(barrier, cells - 1)
        weights_right = remote(weights, weights_left, 14, 1, right)

        @pl.when(has_right)
        def _():
            weights_right.start()

        remote(own_sum, whole, 2, 0, cell).wait_recv()
        fate_right = remote(fates, window.at[pl.ds(0, reach)], 3, 0, right)
        fate_here = remote(fates, window.at[pl.ds(reach, dev_blocks)], 4, 0, cell)
        fate_left = remote(fates, window.at[pl.ds(reach + dev_blocks, reach)], 5, 0, left)


        @pl.when(has_left)
        def _():
            remote(edges.at[0], spare, 13, 0, cell).wait_recv()
            remote(weights, weights_left, 14, 1, left).wait_recv()
            remote(edges.at[1], near_sum.at[0], 1, 0, left).wait_recv()

        @pl.when(jnp.logical_not(has_left))
        def _():
            near_sum[0] = jnp.zeros(near_sum.shape[1:], BF16)
            far_sum[0] = jnp.zeros(far_sum.shape[1:], BF16)
            spare[...] = jnp.zeros(spare.shape, BF16)
            weights_left[...] = jnp.zeros(weights_left.shape, F32)
            far_unit[0] = jnp.zeros((1, height), F32)

        @pl.when(jnp.logical_not(has_right))
        def _():
            near_sum[1] = jnp.zeros(near_sum.shape[1:], BF16)
            far_sum[1] = jnp.zeros(far_sum.shape[1:], BF16)
            far_unit[2] = jnp.zeros((1, height), F32)

        row_sum = jnp.zeros((height, side), F32)
        weighted = jnp.zeros((height, side), F32)
        for r in range(dev_blocks):
            value = whole[r] + near_sum[0, r].astype(F32)
            whole[r] = value
            row_sum = row_sum + value + spare[r].astype(F32)
        mean = jnp.sum(row_sum, axis=1, keepdims=True) * (1.0 / dev_cells)
        per_unit = 1.0 / jnp.where(mean > 0.0, mean, 1.0)
        for r in range(dev_blocks):
            weighted = weighted + whole[r] * per_unit * weights[:, block_range(r)]
            weighted = weighted + spare[r].astype(F32) * per_unit * weights_left[:, block_range(r)]
        remote(first_total, first_total, 11, 0, cell).wait_recv()
        message[:, 0:height] = jnp.sum(weighted.T, axis=0, keepdims=True)
        message[:, height : 2 * height] = jnp.broadcast_to(mean, (height, side)).T[0:1]
        message[:, 2 * height : 3 * height] = first_total[...]

        def tell(step):
            pltpu.make_async_remote_copy(
                src_ref=message, dst_ref=messages.at[cell], send_sem=all_send_sem, recv_sem=all_recv_sem,
                device_id=(1, step + lax.div(step + cells - cell, cells)), device_id_type=MESH,
            ).start()

        for step in range(cells - 1):
            tell(step)

        @pl.when(has_left)
        def _():
            remote(labels.at[0], labels.at[0], 7, 0, left).wait_recv()
            for r in range(reach):
                window[r] = one_hot(labels[0, :, block_range(dev_blocks - reach + r)]).astype(BF16)

        @pl.when(has_right)
        def _():
            remote(labels.at[0], labels.at[2], 8, 0, right).wait_recv()
            for r in range(reach):
                window[reach + dev_blocks + r] = one_hot(labels[2, :, block_range(r)]).astype(BF16)

        for r in range(dev_blocks):
            value = fate_block(r)
            fates[r] = value
            fate_out[0, :, block_range(r)] = value
        @pl.when(has_right)
        def _():
            fate_right.start()

        @pl.when(has_left)
        def _():
            fate_left.start()

        fate_here.start()

        @pl.when(has_right)
        def _():
            remote(edges.at[0], near_sum.at[1], 0, 0, right).wait_recv()

        row_sum = jnp.zeros((height, side), F32)
        for r in range(dev_blocks):
            value = whole[r] + near_sum[1, r].astype(F32)
            whole[r] = value
            row_sum = row_sum + value
        whole_back = remote(whole, whole, 6, 0, cell)
        whole_back.start()
        mean = jnp.sum(row_sum, axis=1, keepdims=True) * (1.0 / dev_cells)
        per_unit = 1.0 / jnp.where(mean > 0.0, mean, 1.0)
        for r in range(dev_blocks):
            scaled[r] = (whole[r] * per_unit * per_growth[:, block_range(r)]).astype(BF16)
        far_unit[1] = jnp.broadcast_to(mean, (height, side)).T[0:1]
        column_sums()
        outer_columns()
        far_left = remote(edges.at[0], far_sum.at[1], 9, 1, left)
        far_right = remote(edges.at[1], far_sum.at[0], 10, 1, right)
        unit_left = remote(far_unit.at[1], far_unit.at[2], 15, 1, left)
        unit_right = remote(far_unit.at[1], far_unit.at[0], 16, 1, right)

        @pl.when(has_right)
        def _():
            unit_right.start()
            far_right.start()

        @pl.when(has_left)
        def _():
            unit_left.start()
            far_left.start()

        own_columns()
        heard = pltpu.make_async_remote_copy(
            src_ref=messages.at[pl.ds(0, cells - 1)], dst_ref=messages.at[pl.ds(0, cells - 1)],
            send_sem=all_send_sem, recv_sem=all_recv_sem, device_id=(1, lax.rem(cell + 1, cells)), device_id_type=MESH,
        )
        heard.wait()
        messages[cell] = message[...]
        first_factor[...] = all_cells / jnp.sum(messages[:, :, 2 * height : 3 * height], axis=0)
        factor_here = remote(first_factor, first_factor, 12, 0, cell)
        factor_here.start()
        sums, units = messages[:, :, 0:height], messages[:, :, height : 2 * height]
        per_largest = 1.0 / jnp.max(units, axis=0)
        common = all_cells / jnp.sum(sums * (units * per_largest), axis=0)
        @pl.when(has_left)
        def _():
            remote(far_unit.at[1], far_unit.at[0], 16, 1, left).wait_recv()
            remote(edges.at[1], far_sum.at[0], 10, 1, left).wait_recv()

        @pl.when(has_right)
        def _():
            remote(far_unit.at[1], far_unit.at[2], 15, 1, right).wait_recv()
            remote(edges.at[0], far_sum.at[1], 9, 1, right).wait_recv()

        factors = [far_unit[i] * per_largest * common for i in range(3)]
        square = jnp.concatenate(factors + [jnp.zeros((height - 3, height), F32)], axis=0).T
        factors = [square[:, i : i + 1] for i in range(3)]
        for r in range(dev_blocks):
            value = own_sum[r] * factors[1] + far_sum[0, r].astype(F32) * factors[0] + far_sum[1, r].astype(F32) * factors[2]
            mass_out[0, :, block_range(r)] = value.astype(BF16)

        @pl.when(has_right)
        def _():
            fate_right.wait_send()
            far_right.wait_send()
            unit_right.wait_send()
            weights_right.wait_send()

        @pl.when(has_left)
        def _():
            fate_left.wait_send()
            far_left.wait_send()
            unit_left.wait_send()

        fate_here.wait_send()
        whole_back.wait_send()
        factor_here.wait_send()


def hand_over(mass, fate, mass_out, fate_out, sems):
    copies = [pltpu.make_async_copy(mass, mass_out, sems.at[0]), pltpu.make_async_copy(fate, fate_out, sems.at[1])]
    for copy in copies:
        copy.start()
    for copy in copies:
        copy.wait()


def on_device(block_rows, block_cols, block_values, growth, first_labels, last_labels):
    slots, side = block_values.shape[1], block_values.shape[2]
    dev_cells = growth.shape[1]
    dev_blocks = dev_cells // side
    panels = first_labels.shape[0]
    height = panels * CELL_TYPES
    cells = lax.axis_size("cell")
    columns = dev_blocks + 2 * BAND_REACH
    steps = (slots + (GROUP - 1) * columns) // GROUP
    out = jax.ShapeDtypeStruct((1, height, dev_cells), BF16)
    copies = 17
    mass, fate = pl.pallas_call(
        kernel,
        out_shape=(out, out),
        in_specs=[pl.BlockSpec(memory_space=pl.ANY)] * 6,
        out_specs=(pl.BlockSpec(memory_space=pltpu.VMEM), pl.BlockSpec(memory_space=pltpu.VMEM)),
        scratch_shapes=[
            pltpu.VMEM((1, slots), jnp.int32),
            pltpu.VMEM((1, slots), jnp.int32),
            pltpu.VMEM((slots, side, side), BF16),
            pltpu.VMEM((1, dev_cells), F32),
            pltpu.VMEM((1, dev_cells), F32),
            pltpu.VMEM((3, panels, dev_cells), jnp.int32),
            pltpu.VMEM((8, 128), jnp.int32),
            pltpu.SMEM((8, 128), jnp.int32),
            pltpu.VMEM((dev_blocks + 1, height, side), BF16),
            pltpu.VMEM((columns, height, side), BF16),
            pltpu.VMEM((steps, height, side), F32),
            pltpu.VMEM((2, BAND_REACH, height, side), BF16),
            pltpu.VMEM((dev_blocks, height, side), F32),
            pltpu.VMEM((dev_blocks, height, side), BF16),
            pltpu.VMEM((2, BAND_REACH, height, side), BF16),
            pltpu.VMEM((2, BAND_REACH, height, side), BF16),
            pltpu.VMEM((BAND_REACH, height, side), BF16),
            pltpu.VMEM((dev_blocks, height, side), F32),
            pltpu.VMEM((1, dev_cells), F32),
            pltpu.VMEM((1, dev_cells), F32),
            pltpu.VMEM((3, 1, height), F32),
            pltpu.VMEM((1, height), F32),
            pltpu.VMEM((1, height), F32),
            pltpu.VMEM((1, 3 * height), F32),
            pltpu.VMEM((cells, 1, 3 * height), F32),
            pltpu.SemaphoreType.DMA((5,)),
            pltpu.SemaphoreType.DMA((4,)),
            pltpu.SemaphoreType.DMA,
            pltpu.SemaphoreType.DMA((copies,)),
            pltpu.SemaphoreType.DMA((copies,)),
            pltpu.SemaphoreType.DMA,
            pltpu.SemaphoreType.DMA,
        ],
        compiler_params=pltpu.CompilerParams(collective_id=0, has_side_effects=True, vmem_limit_bytes=40 * 1024 * 1024),
    )(*[pltpu.with_memory_space_constraint(x, pltpu.HBM) for x in (block_rows, block_cols, block_values, growth, first_labels, last_labels)])
    return pl.pallas_call(
        hand_over,
        out_shape=(out, out),
        in_specs=[pl.BlockSpec(memory_space=pl.ANY)] * 2,
        out_specs=(pl.BlockSpec(memory_space=pl.ANY), pl.BlockSpec(memory_space=pl.ANY)),
        scratch_shapes=[pltpu.SemaphoreType.DMA((2,))],
    )(pltpu.with_memory_space_constraint(mass, pltpu.VMEM), pltpu.with_memory_space_constraint(fate, pltpu.VMEM))


def solution(mesh):
    placed = (
        P("tm", "cell"),
        P("tm", "cell"),
        P("tm", "cell", None, None),
        P("tm", "cell"),
        P(None, "cell"),
        P(None, "cell"),
    )
    return jax.shard_map(
        on_device,
        mesh=mesh,
        in_specs=placed,
        out_specs=(P("tm", None, "cell"), P("tm", None, "cell")),
        check_vma=False,
    )
```

```python
import functools

import jax
import jax.numpy as jnp
from jax import lax
from jax.experimental import pallas as pl
from jax.experimental.pallas import tpu as pltpu
from jax.sharding import PartitionSpec as P

CELL_TYPES = 16
BAND_REACH = 4
GROUP = 2
JOIN = 8
MESH = pl.DeviceIdType.MESH
F32 = jnp.float32
BF16 = jnp.bfloat16


def make_tables(rows, cols, first_block, dev_blocks, per_row, steps, table):
    slots = rows.shape[1]
    lanes = table.shape[1]
    local_row = rows - first_block
    window_col = cols - first_block + BAND_REACH
    down = lax.broadcasted_iota(jnp.int32, (slots, slots), 0)
    across = lax.broadcasted_iota(jnp.int32, (slots, slots), 1)

    def upright(line):
        return jnp.sum(jnp.where(down == across, line, 0), axis=1, keepdims=True)

    row_of, col_of = upright(local_row), upright(window_col)
    earlier = across < down
    in_col = jnp.sum(jnp.where(earlier & (window_col == col_of), 1, 0), axis=1, keepdims=True)
    in_row = jnp.sum(jnp.where(earlier & (local_row == row_of), 1, 0), axis=1, keepdims=True)
    lane = lax.broadcasted_iota(jnp.int32, (slots, lanes), 1)
    slot = lax.broadcasted_iota(jnp.int32, (slots, lanes), 0)
    named = col_of == lane
    count = jnp.sum(jnp.where(named, 1, 0), axis=0, keepdims=True)
    groups = (count + (GROUP - 1)) // GROUP
    base = jnp.sum(jnp.where(lane < col_of, groups, 0), axis=1, keepdims=True)
    place = GROUP * base + in_col
    group_of = base + in_col // GROUP
    hit = place == lane
    group_hit = group_of == lane
    before_hit = group_of == lane - 1
    here = jnp.max(jnp.where(group_hit, col_of, -1), axis=0, keepdims=True)
    before = jnp.max(jnp.where(before_hit, col_of, -2), axis=0, keepdims=True)
    row_place = per_row * row_of + in_row
    row_hit = row_place == lane
    lines = (
        jnp.sum(jnp.where(hit, slot, 0), axis=0, keepdims=True),
        jnp.sum(jnp.where(hit, row_of - dev_blocks, 0), axis=0, keepdims=True) + dev_blocks,
        jnp.where(here == before, 1, 0),
        jnp.max(jnp.where(named, group_of, 0), axis=0, keepdims=True),
        jnp.where(count > 0, 1, 0),
        jnp.sum(jnp.where(row_hit, slot, 0), axis=0, keepdims=True),
        jnp.sum(jnp.where(row_hit, col_of, 0), axis=0, keepdims=True),
        jnp.zeros_like(count),
    )
    bounds = (slots - 1, dev_blocks, 1, steps - 1, 1, slots - 1, dev_blocks + 2 * BAND_REACH - 1, 0)
    lines = [jnp.clip(line, 0, bound) for line, bound in zip(lines, bounds)]
    table[...] = jnp.concatenate(lines, axis=0)


def one_hot(labels):
    panels, side = labels.shape
    kind = lax.broadcasted_iota(jnp.int32, (panels, CELL_TYPES, side), 1)
    marks = jnp.where(labels[:, None, :] == kind, 1.0, 0.0)
    return marks.reshape(panels * CELL_TYPES, side)


def kernel(
    rows_hbm, cols_hbm, blocks_hbm, growth_hbm, first_hbm, last_hbm, mass_out, fate_out,
    rows, cols, blocks, growth, per_growth, labels, table, index, scaled, window, partial, edges, own_sum, fates,
    near_sum, far_sum, spare, whole, part, entire, weights, weights_left, far_unit, first_total, first_factor, message, messages,
    load_sem, block_sem, index_sem, send_sem, recv_sem, all_send_sem, all_recv_sem,
):
    tm, cell = lax.axis_index("tm"), lax.axis_index("cell")
    cells = lax.axis_size("cell")
    right, left = lax.rem(cell + 1, cells), lax.rem(cell + cells - 1, cells)
    has_right, has_left = cell < cells - 1, cell > 0
    slots, side, _ = blocks.shape
    dev_blocks = scaled.shape[0] - 1
    height = scaled.shape[1]
    per_row = slots // dev_blocks
    dev_cells = dev_blocks * side
    all_cells = dev_cells * cells
    reach = BAND_REACH
    steps = partial.shape[0]
    chunks = block_sem.shape[0]
    chunk = slots // chunks

    load_rows = pltpu.make_async_copy(rows_hbm, rows, load_sem.at[0])
    load_cols = pltpu.make_async_copy(cols_hbm, cols, load_sem.at[1])
    load_growth = pltpu.make_async_copy(growth_hbm, growth, load_sem.at[2])
    load_first = pltpu.make_async_copy(first_hbm, labels.at[1], load_sem.at[3])
    load_last = pltpu.make_async_copy(last_hbm, labels.at[1], load_sem.at[3])
    load_passed = pltpu.make_async_copy(last_hbm, labels.at[0], load_sem.at[4])
    load_blocks = [
        pltpu.make_async_copy(blocks_hbm.at[0, pl.ds(i * chunk, chunk)], blocks.at[pl.ds(i * chunk, chunk)], block_sem.at[i])
        for i in range(chunks)
    ]
    barrier = pltpu.get_barrier_semaphore()

    def greet(to_tm, to_cell):
        pl.semaphore_signal(barrier, inc=1, device_id=(to_tm, to_cell), device_id_type=MESH)

    load_rows.start()
    load_cols.start()

    @pl.when(tm == 1)
    def _():
        greet(0, cell)

        @pl.when(has_left)
        def _():
            greet(0, left)

        @pl.when(has_right)
        def _():
            greet(0, right)

    for load in load_blocks:
        load.start()
    load_growth.start()

    @pl.when(tm == 0)
    def _():
        load_first.start()
        load_passed.start()

    @pl.when(tm == 1)
    def _():
        load_last.start()

        def greet_all(step, carry):
            greet(1, lax.rem(cell + step, cells))
            greet(1, lax.rem(cell + cells - step, cells))
            return carry

        lax.fori_loop(1, (cells + 1) // 2, greet_all, 0)
        if cells % 2 == 0:
            greet(1, lax.rem(cell + cells // 2, cells))

    load_rows.wait()
    load_cols.wait()
    make_tables(rows[...], cols[...], cell * dev_blocks, dev_blocks, per_row, steps, table)
    index_copy = pltpu.make_async_copy(table, index, index_sem)
    index_copy.start()

    def remote(source, target, number, to_tm, to_cell):
        return pltpu.make_async_remote_copy(
            src_ref=source, dst_ref=target, send_sem=send_sem.at[number], recv_sem=recv_sem.at[number],
            device_id=(to_tm, to_cell), device_id_type=MESH,
        )

    def block_range(r):
        return pl.ds(r * side, side)

    def column_sums():
        total = None
        for step in range(steps):
            places = [step * GROUP + i for i in range(GROUP)]
            taken = jnp.concatenate([scaled[index[1, p]] for p in places], axis=1)
            stored = jnp.concatenate([blocks[index[0, p]] for p in places], axis=0)
            product = jnp.dot(taken, stored, preferred_element_type=F32)
            if step > 0:
                product = product + jnp.where(index[2, step] > 0, total, 0.0)
            total = product
            partial[step] = total

    def column(w):
        return jnp.where(index[4, w] > 0, partial[index[3, w]], 0.0)

    def outer_columns():
        for w in range(reach):
            edges[0, w] = column(w).astype(BF16)
            edges[1, w] = column(reach + dev_blocks + w).astype(BF16)

    def own_columns():
        for w in range(dev_blocks):
            own_sum[w] = column(reach + w)

    def fate_block(r):
        total = None
        for k in range(0, per_row, JOIN):
            places = [r * per_row + k + i for i in range(JOIN)]
            taken = jnp.concatenate([window[index[6, p]] for p in places], axis=1)
            stored = jnp.concatenate([blocks[index[5, p]] for p in places], axis=1)
            product = lax.dot_general(taken, stored, (((1,), (1,)), ((), ())), preferred_element_type=F32)
            total = product if total is None else total + product
        grouped = total.reshape(height // CELL_TYPES, CELL_TYPES, side)
        grouped = grouped * (CELL_TYPES / jnp.sum(grouped, axis=1, keepdims=True))
        return grouped.reshape(height, side).astype(BF16)

    def row_totals(r):
        ones = jnp.ones((8, JOIN * side), BF16)
        total = None
        for k in range(0, per_row, JOIN):
            places = [r * per_row + k + i for i in range(JOIN)]
            stored = jnp.concatenate([blocks[index[5, p]] for p in places], axis=1)
            product = lax.dot_general(ones, stored, (((1,), (1,)), ((), ())), preferred_element_type=F32)
            total = product if total is None else total + product
        return total[0:1]

    @pl.when(tm == 0)
    def _():
        scaled[dev_blocks] = jnp.zeros((height, side), BF16)
        load_growth.wait()
        load_first.wait()
        for r in range(dev_blocks):
            marks = one_hot(labels[1, :, block_range(r)])
            scaled[r] = (marks / growth[:, block_range(r)]).astype(BF16)
        index_copy.wait()
        for load in load_blocks:
            load.wait()
        column_sums()
        load_passed.wait()
        labels_right = remote(labels.at[0], labels.at[0], 7, 1, right)
        labels_left = remote(labels.at[0], labels.at[2], 8, 1, left)
        edge_left = remote(edges.at[0], near_sum.at[1], 0, 1, left)
        edge_right = remote(edges.at[1], near_sum.at[0], 1, 1, right)
        own_here = remote(own_sum, whole, 2, 1, cell)
        spare_here = remote(edges.at[0], spare, 13, 1, cell)
        total_here = remote(first_total, first_total, 11, 1, cell)
        pl.semaphore_wait(barrier, 2 + lax.div(cell + cells - 1, cells) - lax.div(cell + 1, cells))

        @pl.when(has_right)
        def _():
            labels_right.start()

        @pl.when(has_left)
        def _():
            labels_left.start()

        outer_columns()

        @pl.when(has_right)
        def _():
            edge_right.start()

        @pl.when(has_left)
        def _():
            edge_left.start()
            spare_here.start()

        own_columns()
        own_here.start()
        row_sum = own_sum[0]
        for w in range(1, dev_blocks):
            row_sum = row_sum + own_sum[w]
        for w in range(reach):
            row_sum = row_sum + column(w) + column(reach + dev_blocks + w)
        first_total[...] = jnp.sum(row_sum.T, axis=0, keepdims=True)
        total_here.start()

        @pl.when(has_left)
        def _():
            remote(fates, window.at[pl.ds(0, reach)], 3, 1, left).wait_recv()

        @pl.when(has_right)
        def _():
            remote(fates, window.at[pl.ds(reach + dev_blocks, reach)], 5, 1, right).wait_recv()

        remote(fates, window.at[pl.ds(reach, dev_blocks)], 4, 1, cell).wait_recv()
        for r in range(dev_blocks):
            fate_out[0, :, block_range(r)] = fate_block(r)

        @pl.when(has_right)
        def _():
            edge_right.wait_send()
            labels_right.wait_send()

        @pl.when(has_left)
        def _():
            edge_left.wait_send()
            labels_left.wait_send()
            spare_here.wait_send()

        own_here.wait_send()
        total_here.wait_send()
        remote(whole, whole, 6, 1, cell).wait_recv()
        remote(first_factor, first_factor, 12, 1, cell).wait_recv()
        factor = jnp.broadcast_to(first_factor[...], (height, height)).T
        for r in range(dev_blocks):
            mass_out[0, :, block_range(r)] = (whole[r] * factor).astype(BF16)

    @pl.when(tm == 1)
    def _():
        load_last.wait()
        for r in range(dev_blocks):
            window[reach + r] = one_hot(labels[1, :, block_range(r)]).astype(BF16)
        index_copy.wait()
        for load in load_blocks:
            load.wait()
        totals = [row_totals(r) for r in range(dev_blocks)]
        scaled[dev_blocks] = jnp.zeros((height, side), BF16)
        load_growth.wait()
        per_growth[...] = 1.0 / growth[...]
        for r in range(dev_blocks):
            weights[:, block_range(r)] = totals[r] * per_growth[:, block_range(r)]
        weights_right = remote(weights, weights_left, 14, 1, right)

        fate_right = remote(fates, window.at[pl.ds(0, reach)], 3, 0, right)
        fate_here = remote(fates, window.at[pl.ds(reach, dev_blocks)], 4, 0, cell)
        fate_left = remote(fates, window.at[pl.ds(reach + dev_blocks, reach)], 5, 0, left)


        @pl.when(jnp.logical_not(has_left))
        def _():
            near_sum[0] = jnp.zeros(near_sum.shape[1:], BF16)
            far_sum[0] = jnp.zeros(far_sum.shape[1:], BF16)
            spare[...] = jnp.zeros(spare.shape, BF16)
            weights_left[...] = jnp.zeros(weights_left.shape, F32)
            far_unit[0] = jnp.zeros((1, height), F32)

        @pl.when(jnp.logical_not(has_right))
        def _():
            near_sum[1] = jnp.zeros(near_sum.shape[1:], BF16)
            far_sum[1] = jnp.zeros(far_sum.shape[1:], BF16)
            far_unit[2] = jnp.zeros((1, height), F32)

        def take_left():
            remote(own_sum, whole, 2, 0, cell).wait_recv()

            @pl.when(has_left)
            def _():
                remote(edges.at[1], near_sum.at[0], 1, 0, left).wait_recv()

        def give_weights():
            @pl.when(has_right)
            def _():
                weights_right.start()

        def report():
            @pl.when(has_left)
            def _():
                remote(edges.at[0], spare, 13, 0, cell).wait_recv()
                remote(weights, weights_left, 14, 1, left).wait_recv()

            row_sum = jnp.zeros((height, side), F32)
            weighted = jnp.zeros((height, side), F32)
            for r in range(dev_blocks):
                value = whole[r] + near_sum[0, r].astype(F32)
                part[r] = value
                row_sum = row_sum + value + spare[r].astype(F32)
            mean = jnp.sum(row_sum, axis=1, keepdims=True) * (1.0 / dev_cells)
            per_unit = 1.0 / jnp.where(mean > 0.0, mean, 1.0)
            for r in range(dev_blocks):
                weighted = weighted + part[r] * per_unit * weights[:, block_range(r)]
                weighted = weighted + spare[r].astype(F32) * per_unit * weights_left[:, block_range(r)]
            remote(first_total, first_total, 11, 0, cell).wait_recv()
            message[:, 0:height] = jnp.sum(weighted.T, axis=0, keepdims=True)
            message[:, height : 2 * height] = jnp.broadcast_to(mean, (height, side)).T[0:1]
            message[:, 2 * height : 3 * height] = first_total[...]

            def tell(step):
                pltpu.make_async_remote_copy(
                    src_ref=message, dst_ref=messages.at[cell], send_sem=all_send_sem, recv_sem=all_recv_sem,
                    device_id=(1, step + lax.div(step + cells - cell, cells)), device_id_type=MESH,
                ).start()

            for step in range(cells - 1):
                tell(step)

        def go_back():
            @pl.when(has_left)
            def _():
                remote(labels.at[0], labels.at[0], 7, 0, left).wait_recv()
                for r in range(reach):
                    window[r] = one_hot(labels[0, :, block_range(dev_blocks - reach + r)]).astype(BF16)

            @pl.when(has_right)
            def _():
                remote(labels.at[0], labels.at[2], 8, 0, right).wait_recv()
                for r in range(reach):
                    window[reach + dev_blocks + r] = one_hot(labels[2, :, block_range(r)]).astype(BF16)

            for r in range(dev_blocks):
                value = fate_block(r)
                fates[r] = value
                fate_out[0, :, block_range(r)] = value
            @pl.when(has_right)
            def _():
                fate_right.start()

            @pl.when(has_left)
            def _():
                fate_left.start()

            fate_here.start()

        early = (cell < 13) | (cell == 16)

        @pl.when(jnp.logical_not(early))
        def _():
            pl.semaphore_wait(barrier, cells - 1)
            give_weights()
            take_left()
            report()
            go_back()

        @pl.when(has_right)
        def _():
            remote(edges.at[0], near_sum.at[1], 0, 0, right).wait_recv()

        @pl.when(early)
        def _():
            give_weights()
            take_left()

        row_sum = jnp.zeros((height, side), F32)
        for r in range(dev_blocks):
            value = whole[r] + near_sum[0, r].astype(F32) + near_sum[1, r].astype(F32)
            entire[r] = value
            row_sum = row_sum + value
        whole_back = remote(entire, whole, 6, 0, cell)
        whole_back.start()
        mean = jnp.sum(row_sum, axis=1, keepdims=True) * (1.0 / dev_cells)
        per_unit = 1.0 / jnp.where(mean > 0.0, mean, 1.0)
        for r in range(dev_blocks):
            scaled[r] = (entire[r] * per_unit * per_growth[:, block_range(r)]).astype(BF16)
        far_unit[1] = jnp.broadcast_to(mean, (height, side)).T[0:1]
        column_sums()
        outer_columns()
        far_left = remote(edges.at[0], far_sum.at[1], 9, 1, left)
        far_right = remote(edges.at[1], far_sum.at[0], 10, 1, right)
        unit_left = remote(far_unit.at[1], far_unit.at[2], 15, 1, left)
        unit_right = remote(far_unit.at[1], far_unit.at[0], 16, 1, right)

        @pl.when(has_right)
        def _():
            unit_right.start()
            far_right.start()

        @pl.when(has_left)
        def _():
            unit_left.start()
            far_left.start()

        own_columns()

        @pl.when(early)
        def _():
            pl.semaphore_wait(barrier, cells - 1)
            report()
            go_back()

        heard = pltpu.make_async_remote_copy(
            src_ref=messages.at[pl.ds(0, cells - 1)], dst_ref=messages.at[pl.ds(0, cells - 1)],
            send_sem=all_send_sem, recv_sem=all_recv_sem, device_id=(1, lax.rem(cell + 1, cells)), device_id_type=MESH,
        )
        heard.wait()
        messages[cell] = message[...]
        first_factor[...] = all_cells / jnp.sum(messages[:, :, 2 * height : 3 * height], axis=0)
        factor_here = remote(first_factor, first_factor, 12, 0, cell)
        factor_here.start()
        sums, units = messages[:, :, 0:height], messages[:, :, height : 2 * height]
        per_largest = 1.0 / jnp.max(units, axis=0)
        common = all_cells / jnp.sum(sums * (units * per_largest), axis=0)
        @pl.when(has_left)
        def _():
            remote(far_unit.at[1], far_unit.at[0], 16, 1, left).wait_recv()
            remote(edges.at[1], far_sum.at[0], 10, 1, left).wait_recv()

        @pl.when(has_right)
        def _():
            remote(far_unit.at[1], far_unit.at[2], 15, 1, right).wait_recv()
            remote(edges.at[0], far_sum.at[1], 9, 1, right).wait_recv()

        factors = [far_unit[i] * per_largest * common for i in range(3)]
        square = jnp.concatenate(factors + [jnp.zeros((height - 3, height), F32)], axis=0).T
        factors = [square[:, i : i + 1] for i in range(3)]
        for r in range(dev_blocks):
            value = own_sum[r] * factors[1] + far_sum[0, r].astype(F32) * factors[0] + far_sum[1, r].astype(F32) * factors[2]
            mass_out[0, :, block_range(r)] = value.astype(BF16)

        @pl.when(has_right)
        def _():
            fate_right.wait_send()
            far_right.wait_send()
            unit_right.wait_send()
            weights_right.wait_send()

        @pl.when(has_left)
        def _():
            fate_left.wait_send()
            far_left.wait_send()
            unit_left.wait_send()

        fate_here.wait_send()
        whole_back.wait_send()
        factor_here.wait_send()


def hand_over(mass, fate, mass_out, fate_out, sems):
    copies = [pltpu.make_async_copy(mass, mass_out, sems.at[0]), pltpu.make_async_copy(fate, fate_out, sems.at[1])]
    for copy in copies:
        copy.start()
    for copy in copies:
        copy.wait()


def on_device(block_rows, block_cols, block_values, growth, first_labels, last_labels):
    slots, side = block_values.shape[1], block_values.shape[2]
    dev_cells = growth.shape[1]
    dev_blocks = dev_cells // side
    panels = first_labels.shape[0]
    height = panels * CELL_TYPES
    cells = lax.axis_size("cell")
    columns = dev_blocks + 2 * BAND_REACH
    steps = (slots + (GROUP - 1) * columns) // GROUP
    out = jax.ShapeDtypeStruct((1, height, dev_cells), BF16)
    copies = 17
    mass, fate = pl.pallas_call(
        kernel,
        out_shape=(out, out),
        in_specs=[pl.BlockSpec(memory_space=pl.ANY)] * 6,
        out_specs=(pl.BlockSpec(memory_space=pltpu.VMEM), pl.BlockSpec(memory_space=pltpu.VMEM)),
        scratch_shapes=[
            pltpu.VMEM((1, slots), jnp.int32),
            pltpu.VMEM((1, slots), jnp.int32),
            pltpu.VMEM((slots, side, side), BF16),
            pltpu.VMEM((1, dev_cells), F32),
            pltpu.VMEM((1, dev_cells), F32),
            pltpu.VMEM((3, panels, dev_cells), jnp.int32),
            pltpu.VMEM((8, 128), jnp.int32),
            pltpu.SMEM((8, 128), jnp.int32),
            pltpu.VMEM((dev_blocks + 1, height, side), BF16),
            pltpu.VMEM((columns, height, side), BF16),
            pltpu.VMEM((steps, height, side), F32),
            pltpu.VMEM((2, BAND_REACH, height, side), BF16),
            pltpu.VMEM((dev_blocks, height, side), F32),
            pltpu.VMEM((dev_blocks, height, side), BF16),
            pltpu.VMEM((2, BAND_REACH, height, side), BF16),
            pltpu.VMEM((2, BAND_REACH, height, side), BF16),
            pltpu.VMEM((BAND_REACH, height, side), BF16),
            pltpu.VMEM((dev_blocks, height, side), F32),
            pltpu.VMEM((dev_blocks, height, side), F32),
            pltpu.VMEM((dev_blocks, height, side), F32),
            pltpu.VMEM((1, dev_cells), F32),
            pltpu.VMEM((1, dev_cells), F32),
            pltpu.VMEM((3, 1, height), F32),
            pltpu.VMEM((1, height), F32),
            pltpu.VMEM((1, height), F32),
            pltpu.VMEM((1, 3 * height), F32),
            pltpu.VMEM((cells, 1, 3 * height), F32),
            pltpu.SemaphoreType.DMA((5,)),
            pltpu.SemaphoreType.DMA((4,)),
            pltpu.SemaphoreType.DMA,
            pltpu.SemaphoreType.DMA((copies,)),
            pltpu.SemaphoreType.DMA((copies,)),
            pltpu.SemaphoreType.DMA,
            pltpu.SemaphoreType.DMA,
        ],
        compiler_params=pltpu.CompilerParams(collective_id=0, has_side_effects=True, vmem_limit_bytes=40 * 1024 * 1024),
    )(*[pltpu.with_memory_space_constraint(x, pltpu.HBM) for x in (block_rows, block_cols, block_values, growth, first_labels, last_labels)])
    return pl.pallas_call(
        hand_over,
        out_shape=(out, out),
        in_specs=[pl.BlockSpec(memory_space=pl.ANY)] * 2,
        out_specs=(pl.BlockSpec(memory_space=pl.ANY), pl.BlockSpec(memory_space=pl.ANY)),
        scratch_shapes=[pltpu.SemaphoreType.DMA((2,))],
    )(pltpu.with_memory_space_constraint(mass, pltpu.VMEM), pltpu.with_memory_space_constraint(fate, pltpu.VMEM))


def solution(mesh):
    placed = (
        P("tm", "cell"),
        P("tm", "cell"),
        P("tm", "cell", None, None),
        P("tm", "cell"),
        P(None, "cell"),
        P(None, "cell"),
    )
    return jax.shard_map(
        on_device,
        mesh=mesh,
        in_specs=placed,
        out_specs=(P("tm", None, "cell"), P("tm", None, "cell")),
        check_vma=False,
    )
```

```python
import functools

import jax
import jax.numpy as jnp
from jax import lax
from jax.experimental import pallas as pl
from jax.experimental.pallas import tpu as pltpu
from jax.sharding import PartitionSpec as P

CELL_TYPES = 16
BAND_REACH = 4
GROUP = 2
JOIN = 8
MESH = pl.DeviceIdType.MESH
F32 = jnp.float32
BF16 = jnp.bfloat16


def make_tables(rows, cols, first_block, dev_blocks, per_row, steps, table):
    slots = rows.shape[1]
    lanes = table.shape[1]
    local_row = rows - first_block
    window_col = cols - first_block + BAND_REACH
    down = lax.broadcasted_iota(jnp.int32, (slots, slots), 0)
    across = lax.broadcasted_iota(jnp.int32, (slots, slots), 1)

    def upright(line):
        return jnp.sum(jnp.where(down == across, line, 0), axis=1, keepdims=True)

    row_of, col_of = upright(local_row), upright(window_col)
    earlier = across < down
    in_col = jnp.sum(jnp.where(earlier & (window_col == col_of), 1, 0), axis=1, keepdims=True)
    in_row = jnp.sum(jnp.where(earlier & (local_row == row_of), 1, 0), axis=1, keepdims=True)
    lane = lax.broadcasted_iota(jnp.int32, (slots, lanes), 1)
    slot = lax.broadcasted_iota(jnp.int32, (slots, lanes), 0)
    named = col_of == lane
    count = jnp.sum(jnp.where(named, 1, 0), axis=0, keepdims=True)
    groups = (count + (GROUP - 1)) // GROUP
    base = jnp.sum(jnp.where(lane < col_of, groups, 0), axis=1, keepdims=True)
    place = GROUP * base + in_col
    group_of = base + in_col // GROUP
    hit = place == lane
    group_hit = group_of == lane
    before_hit = group_of == lane - 1
    here = jnp.max(jnp.where(group_hit, col_of, -1), axis=0, keepdims=True)
    before = jnp.max(jnp.where(before_hit, col_of, -2), axis=0, keepdims=True)
    row_place = per_row * row_of + in_row
    row_hit = row_place == lane
    lines = (
        jnp.sum(jnp.where(hit, slot, 0), axis=0, keepdims=True),
        jnp.sum(jnp.where(hit, row_of - dev_blocks, 0), axis=0, keepdims=True) + dev_blocks,
        jnp.where(here == before, 1, 0),
        jnp.max(jnp.where(named, group_of, 0), axis=0, keepdims=True),
        jnp.where(count > 0, 1, 0),
        jnp.sum(jnp.where(row_hit, slot, 0), axis=0, keepdims=True),
        jnp.sum(jnp.where(row_hit, col_of, 0), axis=0, keepdims=True),
        jnp.zeros_like(count),
    )
    bounds = (slots - 1, dev_blocks, 1, steps - 1, 1, slots - 1, dev_blocks + 2 * BAND_REACH - 1, 0)
    lines = [jnp.clip(line, 0, bound) for line, bound in zip(lines, bounds)]
    table[...] = jnp.concatenate(lines, axis=0)


def one_hot(labels):
    panels, side = labels.shape
    kind = lax.broadcasted_iota(jnp.int32, (panels, CELL_TYPES, side), 1)
    marks = jnp.where(labels[:, None, :] == kind, 1.0, 0.0)
    return marks.reshape(panels * CELL_TYPES, side)


def kernel(
    rows_hbm, cols_hbm, blocks_hbm, growth_hbm, first_hbm, last_hbm, mass_out, fate_out,
    rows, cols, blocks, growth, per_growth, labels, table, index, scaled, window, partial, edges, own_sum, fates,
    near_sum, far_sum, spare, whole, part, entire, weights, weights_left, far_unit, first_total, first_factor, message, messages,
    load_sem, block_sem, index_sem, send_sem, recv_sem, all_send_sem, all_recv_sem,
):
    tm, cell = lax.axis_index("tm"), lax.axis_index("cell")
    cells = lax.axis_size("cell")
    right, left = lax.rem(cell + 1, cells), lax.rem(cell + cells - 1, cells)
    has_right, has_left = cell < cells - 1, cell > 0
    slots, side, _ = blocks.shape
    dev_blocks = scaled.shape[0] - 1
    height = scaled.shape[1]
    per_row = slots // dev_blocks
    dev_cells = dev_blocks * side
    all_cells = dev_cells * cells
    reach = BAND_REACH
    steps = partial.shape[0]
    chunks = block_sem.shape[0]
    chunk = slots // chunks

    load_rows = pltpu.make_async_copy(rows_hbm, rows, load_sem.at[0])
    load_cols = pltpu.make_async_copy(cols_hbm, cols, load_sem.at[1])
    load_growth = pltpu.make_async_copy(growth_hbm, growth, load_sem.at[2])
    load_first = pltpu.make_async_copy(first_hbm, labels.at[1], load_sem.at[3])
    load_last = pltpu.make_async_copy(last_hbm, labels.at[1], load_sem.at[3])
    load_passed = pltpu.make_async_copy(last_hbm, labels.at[0], load_sem.at[4])
    load_blocks = [
        pltpu.make_async_copy(blocks_hbm.at[0, pl.ds(i * chunk, chunk)], blocks.at[pl.ds(i * chunk, chunk)], block_sem.at[i])
        for i in range(chunks)
    ]
    barrier = pltpu.get_barrier_semaphore()

    def greet(to_tm, to_cell):
        pl.semaphore_signal(barrier, inc=1, device_id=(to_tm, to_cell), device_id_type=MESH)

    load_rows.start()
    load_cols.start()

    @pl.when(tm == 1)
    def _():
        greet(0, cell)

        @pl.when(has_left)
        def _():
            greet(0, left)

        @pl.when(has_right)
        def _():
            greet(0, right)

    for load in load_blocks:
        load.start()
    load_growth.start()

    @pl.when(tm == 0)
    def _():
        load_first.start()
        load_passed.start()

    @pl.when(tm == 1)
    def _():
        load_last.start()

        def greet_all(step, carry):
            greet(1, lax.rem(cell + step, cells))
            greet(1, lax.rem(cell + cells - step, cells))
            return carry

        lax.fori_loop(1, (cells + 1) // 2, greet_all, 0)
        if cells % 2 == 0:
            greet(1, lax.rem(cell + cells // 2, cells))

    load_rows.wait()
    load_cols.wait()
    make_tables(rows[...], cols[...], cell * dev_blocks, dev_blocks, per_row, steps, table)
    index_copy = pltpu.make_async_copy(table, index, index_sem)
    index_copy.start()

    def remote(source, target, number, to_tm, to_cell):
        return pltpu.make_async_remote_copy(
            src_ref=source, dst_ref=target, send_sem=send_sem.at[number], recv_sem=recv_sem.at[number],
            device_id=(to_tm, to_cell), device_id_type=MESH,
        )

    def block_range(r):
        return pl.ds(r * side, side)

    def column_sums():
        total = None
        for step in range(steps):
            places = [step * GROUP + i for i in range(GROUP)]
            taken = jnp.concatenate([scaled[index[1, p]] for p in places], axis=1)
            stored = jnp.concatenate([blocks[index[0, p]] for p in places], axis=0)
            product = jnp.dot(taken, stored, preferred_element_type=F32)
            if step > 0:
                product = product + jnp.where(index[2, step] > 0, total, 0.0)
            total = product
            partial[step] = total

    def column(w):
        return jnp.where(index[4, w] > 0, partial[index[3, w]], 0.0)

    def outer_columns():
        for w in range(reach):
            edges[0, w] = column(w).astype(BF16)
            edges[1, w] = column(reach + dev_blocks + w).astype(BF16)

    def own_columns():
        for w in range(dev_blocks):
            own_sum[w] = column(reach + w)

    def fate_block(r):
        total = None
        for k in range(0, per_row, JOIN):
            places = [r * per_row + k + i for i in range(JOIN)]
            taken = jnp.concatenate([window[index[6, p]] for p in places], axis=1)
            stored = jnp.concatenate([blocks[index[5, p]] for p in places], axis=1)
            product = lax.dot_general(taken, stored, (((1,), (1,)), ((), ())), preferred_element_type=F32)
            total = product if total is None else total + product
        grouped = total.reshape(height // CELL_TYPES, CELL_TYPES, side)
        grouped = grouped * (CELL_TYPES / jnp.sum(grouped, axis=1, keepdims=True))
        return grouped.reshape(height, side).astype(BF16)

    def row_totals(r):
        ones = jnp.ones((8, JOIN * side), BF16)
        total = None
        for k in range(0, per_row, JOIN):
            places = [r * per_row + k + i for i in range(JOIN)]
            stored = jnp.concatenate([blocks[index[5, p]] for p in places], axis=1)
            product = lax.dot_general(ones, stored, (((1,), (1,)), ((), ())), preferred_element_type=F32)
            total = product if total is None else total + product
        return total[0:1]

    @pl.when(tm == 0)
    def _():
        scaled[dev_blocks] = jnp.zeros((height, side), BF16)
        load_growth.wait()
        load_first.wait()
        for r in range(dev_blocks):
            marks = one_hot(labels[1, :, block_range(r)])
            scaled[r] = (marks / growth[:, block_range(r)]).astype(BF16)
        index_copy.wait()
        for load in load_blocks:
            load.wait()
        column_sums()
        load_passed.wait()
        labels_right = remote(labels.at[0], labels.at[0], 7, 1, right)
        labels_left = remote(labels.at[0], labels.at[2], 8, 1, left)
        edge_left = remote(edges.at[0], near_sum.at[1], 0, 1, left)
        edge_right = remote(edges.at[1], near_sum.at[0], 1, 1, right)
        own_here = remote(own_sum, whole, 2, 1, cell)
        spare_here = remote(edges.at[0], spare, 13, 1, cell)
        total_here = remote(first_total, first_total, 11, 1, cell)
        pl.semaphore_wait(barrier, 2 + lax.div(cell + cells - 1, cells) - lax.div(cell + 1, cells))

        @pl.when(has_right)
        def _():
            labels_right.start()

        @pl.when(has_left)
        def _():
            labels_left.start()

        outer_columns()

        @pl.when(has_right)
        def _():
            edge_right.start()

        @pl.when(has_left)
        def _():
            edge_left.start()

        own_columns()
        own_here.start()

        @pl.when(has_left)
        def _():
            spare_here.start()

        row_sum = own_sum[0]
        for w in range(1, dev_blocks):
            row_sum = row_sum + own_sum[w]
        for w in range(reach):
            row_sum = row_sum + column(w) + column(reach + dev_blocks + w)
        first_total[...] = jnp.sum(row_sum.T, axis=0, keepdims=True)
        total_here.start()

        @pl.when(has_left)
        def _():
            remote(fates, window.at[pl.ds(0, reach)], 3, 1, left).wait_recv()

        @pl.when(has_right)
        def _():
            remote(fates, window.at[pl.ds(reach + dev_blocks, reach)], 5, 1, right).wait_recv()

        remote(fates, window.at[pl.ds(reach, dev_blocks)], 4, 1, cell).wait_recv()
        for r in range(dev_blocks):
            fate_out[0, :, block_range(r)] = fate_block(r)

        @pl.when(has_right)
        def _():
            edge_right.wait_send()
            labels_right.wait_send()

        @pl.when(has_left)
        def _():
            edge_left.wait_send()
            labels_left.wait_send()
            spare_here.wait_send()

        own_here.wait_send()
        total_here.wait_send()
        remote(whole, whole, 6, 1, cell).wait_recv()
        remote(first_factor, first_factor, 12, 1, cell).wait_recv()
        factor = jnp.broadcast_to(first_factor[...], (height, height)).T
        for r in range(dev_blocks):
            mass_out[0, :, block_range(r)] = (whole[r] * factor).astype(BF16)

    @pl.when(tm == 1)
    def _():
        load_last.wait()
        for r in range(dev_blocks):
            window[reach + r] = one_hot(labels[1, :, block_range(r)]).astype(BF16)
        index_copy.wait()
        for load in load_blocks:
            load.wait()
        totals = [row_totals(r) for r in range(dev_blocks)]
        scaled[dev_blocks] = jnp.zeros((height, side), BF16)
        load_growth.wait()
        per_growth[...] = 1.0 / growth[...]
        for r in range(dev_blocks):
            weights[:, block_range(r)] = totals[r] * per_growth[:, block_range(r)]
        weights_right = remote(weights, weights_left, 14, 1, right)

        fate_right = remote(fates, window.at[pl.ds(0, reach)], 3, 0, right)
        fate_here = remote(fates, window.at[pl.ds(reach, dev_blocks)], 4, 0, cell)
        fate_left = remote(fates, window.at[pl.ds(reach + dev_blocks, reach)], 5, 0, left)


        @pl.when(jnp.logical_not(has_left))
        def _():
            near_sum[0] = jnp.zeros(near_sum.shape[1:], BF16)
            far_sum[0] = jnp.zeros(far_sum.shape[1:], BF16)
            spare[...] = jnp.zeros(spare.shape, BF16)
            weights_left[...] = jnp.zeros(weights_left.shape, F32)
            far_unit[0] = jnp.zeros((1, height), F32)

        @pl.when(jnp.logical_not(has_right))
        def _():
            near_sum[1] = jnp.zeros(near_sum.shape[1:], BF16)
            far_sum[1] = jnp.zeros(far_sum.shape[1:], BF16)
            far_unit[2] = jnp.zeros((1, height), F32)

        def take_left():
            remote(own_sum, whole, 2, 0, cell).wait_recv()

            @pl.when(has_left)
            def _():
                remote(edges.at[1], near_sum.at[0], 1, 0, left).wait_recv()

        def give_weights():
            @pl.when(has_right)
            def _():
                weights_right.start()

        def report():
            @pl.when(has_left)
            def _():
                remote(edges.at[0], spare, 13, 0, cell).wait_recv()
                remote(weights, weights_left, 14, 1, left).wait_recv()

            row_sum = jnp.zeros((height, side), F32)
            weighted = jnp.zeros((height, side), F32)
            for r in range(dev_blocks):
                value = whole[r] + near_sum[0, r].astype(F32)
                part[r] = value
                row_sum = row_sum + value + spare[r].astype(F32)
            mean = jnp.sum(row_sum, axis=1, keepdims=True) * (1.0 / dev_cells)
            per_unit = 1.0 / jnp.where(mean > 0.0, mean, 1.0)
            for r in range(dev_blocks):
                weighted = weighted + part[r] * per_unit * weights[:, block_range(r)]
                weighted = weighted + spare[r].astype(F32) * per_unit * weights_left[:, block_range(r)]
            remote(first_total, first_total, 11, 0, cell).wait_recv()
            message[:, 0:height] = jnp.sum(weighted.T, axis=0, keepdims=True)
            message[:, height : 2 * height] = jnp.broadcast_to(mean, (height, side)).T[0:1]
            message[:, 2 * height : 3 * height] = first_total[...]

            def tell(step):
                pltpu.make_async_remote_copy(
                    src_ref=message, dst_ref=messages.at[cell], send_sem=all_send_sem, recv_sem=all_recv_sem,
                    device_id=(1, step + lax.div(step + cells - cell, cells)), device_id_type=MESH,
                ).start()

            for step in range(cells - 1):
                tell(step)

        def go_back():
            @pl.when(has_left)
            def _():
                remote(labels.at[0], labels.at[0], 7, 0, left).wait_recv()
                for r in range(reach):
                    window[r] = one_hot(labels[0, :, block_range(dev_blocks - reach + r)]).astype(BF16)

            @pl.when(has_right)
            def _():
                remote(labels.at[0], labels.at[2], 8, 0, right).wait_recv()
                for r in range(reach):
                    window[reach + dev_blocks + r] = one_hot(labels[2, :, block_range(r)]).astype(BF16)

            for r in range(dev_blocks):
                value = fate_block(r)
                fates[r] = value
                fate_out[0, :, block_range(r)] = value
            @pl.when(has_right)
            def _():
                fate_right.start()

            @pl.when(has_left)
            def _():
                fate_left.start()

            fate_here.start()

        early = (cell < 13) | (cell == 16)

        @pl.when(jnp.logical_not(early))
        def _():
            pl.semaphore_wait(barrier, cells - 1)
            give_weights()
            take_left()
            report()
            go_back()

        @pl.when(has_right)
        def _():
            remote(edges.at[0], near_sum.at[1], 0, 0, right).wait_recv()

        @pl.when(early)
        def _():
            give_weights()
            take_left()

        row_sum = jnp.zeros((height, side), F32)
        for r in range(dev_blocks):
            value = whole[r] + near_sum[0, r].astype(F32) + near_sum[1, r].astype(F32)
            entire[r] = value
            row_sum = row_sum + value
        whole_back = remote(entire, whole, 6, 0, cell)
        whole_back.start()
        mean = jnp.sum(row_sum, axis=1, keepdims=True) * (1.0 / dev_cells)
        per_unit = 1.0 / jnp.where(mean > 0.0, mean, 1.0)
        for r in range(dev_blocks):
            scaled[r] = (entire[r] * per_unit * per_growth[:, block_range(r)]).astype(BF16)
        far_unit[1] = jnp.broadcast_to(mean, (height, side)).T[0:1]
        column_sums()
        outer_columns()
        far_left = remote(edges.at[0], far_sum.at[1], 9, 1, left)
        far_right = remote(edges.at[1], far_sum.at[0], 10, 1, right)
        unit_left = remote(far_unit.at[1], far_unit.at[2], 15, 1, left)
        unit_right = remote(far_unit.at[1], far_unit.at[0], 16, 1, right)

        @pl.when(has_right)
        def _():
            unit_right.start()
            far_right.start()

        @pl.when(has_left)
        def _():
            unit_left.start()
            far_left.start()

        own_columns()

        @pl.when(early)
        def _():
            pl.semaphore_wait(barrier, cells - 1)
            report()
            go_back()

        heard = pltpu.make_async_remote_copy(
            src_ref=messages.at[pl.ds(0, cells - 1)], dst_ref=messages.at[pl.ds(0, cells - 1)],
            send_sem=all_send_sem, recv_sem=all_recv_sem, device_id=(1, lax.rem(cell + 1, cells)), device_id_type=MESH,
        )
        heard.wait()
        messages[cell] = message[...]
        first_factor[...] = all_cells / jnp.sum(messages[:, :, 2 * height : 3 * height], axis=0)
        factor_here = remote(first_factor, first_factor, 12, 0, cell)
        factor_here.start()
        sums, units = messages[:, :, 0:height], messages[:, :, height : 2 * height]
        per_largest = 1.0 / jnp.max(units, axis=0)
        common = all_cells / jnp.sum(sums * (units * per_largest), axis=0)
        @pl.when(has_left)
        def _():
            remote(far_unit.at[1], far_unit.at[0], 16, 1, left).wait_recv()
            remote(edges.at[1], far_sum.at[0], 10, 1, left).wait_recv()

        @pl.when(has_right)
        def _():
            remote(far_unit.at[1], far_unit.at[2], 15, 1, right).wait_recv()
            remote(edges.at[0], far_sum.at[1], 9, 1, right).wait_recv()

        factors = [far_unit[i] * per_largest * common for i in range(3)]
        square = jnp.concatenate(factors + [jnp.zeros((height - 3, height), F32)], axis=0).T
        factors = [square[:, i : i + 1] for i in range(3)]
        for r in range(dev_blocks):
            value = own_sum[r] * factors[1] + far_sum[0, r].astype(F32) * factors[0] + far_sum[1, r].astype(F32) * factors[2]
            mass_out[0, :, block_range(r)] = value.astype(BF16)

        @pl.when(has_right)
        def _():
            fate_right.wait_send()
            far_right.wait_send()
            unit_right.wait_send()
            weights_right.wait_send()

        @pl.when(has_left)
        def _():
            fate_left.wait_send()
            far_left.wait_send()
            unit_left.wait_send()

        fate_here.wait_send()
        whole_back.wait_send()
        factor_here.wait_send()


def hand_over(mass, fate, mass_out, fate_out, sems):
    copies = [pltpu.make_async_copy(mass, mass_out, sems.at[0]), pltpu.make_async_copy(fate, fate_out, sems.at[1])]
    for copy in copies:
        copy.start()
    for copy in copies:
        copy.wait()


def on_device(block_rows, block_cols, block_values, growth, first_labels, last_labels):
    slots, side = block_values.shape[1], block_values.shape[2]
    dev_cells = growth.shape[1]
    dev_blocks = dev_cells // side
    panels = first_labels.shape[0]
    height = panels * CELL_TYPES
    cells = lax.axis_size("cell")
    columns = dev_blocks + 2 * BAND_REACH
    steps = (slots + (GROUP - 1) * columns) // GROUP
    out = jax.ShapeDtypeStruct((1, height, dev_cells), BF16)
    copies = 17
    mass, fate = pl.pallas_call(
        kernel,
        out_shape=(out, out),
        in_specs=[pl.BlockSpec(memory_space=pl.ANY)] * 6,
        out_specs=(pl.BlockSpec(memory_space=pltpu.VMEM), pl.BlockSpec(memory_space=pltpu.VMEM)),
        scratch_shapes=[
            pltpu.VMEM((1, slots), jnp.int32),
            pltpu.VMEM((1, slots), jnp.int32),
            pltpu.VMEM((slots, side, side), BF16),
            pltpu.VMEM((1, dev_cells), F32),
            pltpu.VMEM((1, dev_cells), F32),
            pltpu.VMEM((3, panels, dev_cells), jnp.int32),
            pltpu.VMEM((8, 128), jnp.int32),
            pltpu.SMEM((8, 128), jnp.int32),
            pltpu.VMEM((dev_blocks + 1, height, side), BF16),
            pltpu.VMEM((columns, height, side), BF16),
            pltpu.VMEM((steps, height, side), F32),
            pltpu.VMEM((2, BAND_REACH, height, side), BF16),
            pltpu.VMEM((dev_blocks, height, side), F32),
            pltpu.VMEM((dev_blocks, height, side), BF16),
            pltpu.VMEM((2, BAND_REACH, height, side), BF16),
            pltpu.VMEM((2, BAND_REACH, height, side), BF16),
            pltpu.VMEM((BAND_REACH, height, side), BF16),
            pltpu.VMEM((dev_blocks, height, side), F32),
            pltpu.VMEM((dev_blocks, height, side), F32),
            pltpu.VMEM((dev_blocks, height, side), F32),
            pltpu.VMEM((1, dev_cells), F32),
            pltpu.VMEM((1, dev_cells), F32),
            pltpu.VMEM((3, 1, height), F32),
            pltpu.VMEM((1, height), F32),
            pltpu.VMEM((1, height), F32),
            pltpu.VMEM((1, 3 * height), F32),
            pltpu.VMEM((cells, 1, 3 * height), F32),
            pltpu.SemaphoreType.DMA((5,)),
            pltpu.SemaphoreType.DMA((4,)),
            pltpu.SemaphoreType.DMA,
            pltpu.SemaphoreType.DMA((copies,)),
            pltpu.SemaphoreType.DMA((copies,)),
            pltpu.SemaphoreType.DMA,
            pltpu.SemaphoreType.DMA,
        ],
        compiler_params=pltpu.CompilerParams(collective_id=0, has_side_effects=True, vmem_limit_bytes=40 * 1024 * 1024),
    )(*[pltpu.with_memory_space_constraint(x, pltpu.HBM) for x in (block_rows, block_cols, block_values, growth, first_labels, last_labels)])
    return pl.pallas_call(
        hand_over,
        out_shape=(out, out),
        in_specs=[pl.BlockSpec(memory_space=pl.ANY)] * 2,
        out_specs=(pl.BlockSpec(memory_space=pl.ANY), pl.BlockSpec(memory_space=pl.ANY)),
        scratch_shapes=[pltpu.SemaphoreType.DMA((2,))],
    )(pltpu.with_memory_space_constraint(mass, pltpu.VMEM), pltpu.with_memory_space_constraint(fate, pltpu.VMEM))


def solution(mesh):
    placed = (
        P("tm", "cell"),
        P("tm", "cell"),
        P("tm", "cell", None, None),
        P("tm", "cell"),
        P(None, "cell"),
        P(None, "cell"),
    )
    return jax.shard_map(
        on_device,
        mesh=mesh,
        in_specs=placed,
        out_specs=(P("tm", None, "cell"), P("tm", None, "cell")),
        check_vma=False,
    )
```
